256 devices in a mesh: rows: 8 (over y, core), cols: 32 (over z, x).
Axes of the slice: x: 4, y: 4, z: 8, core: 2. Of those that a mesh axis runs over, the one named last changes fastest.
Arguments:
- band_input: bfloat16 [512, 1024, 512], P('rows', 'cols'), may hold values from -1000 to 1000
- column_taps: float32 [21, 512], replicated, may hold values from -1 to 1
- row_taps: float32 [21, 512], replicated, may hold values from -1 to 1
- w_squeeze: bfloat16 [512, 512], replicated, may hold values from -0.25 to 0.25
- bases_init: float32 [512, 64], replicated, may hold values from 0.004 to 0.12
- w_ham: bfloat16 [512, 512], replicated, may hold values from -0.25 to 0.25
- w_align: bfloat16 [512, 512], replicated, may hold values from -0.25 to 0.25
Outputs:
- head_out: bfloat16 [512, 1024, 512], P('rows', 'cols')
The draws below stay inside these ranges and needn't reach their ends.
All inputs are finite; a program needn't handle non-finite values.
Results may differ from the reference program's by a relative error of at most 0.0071.
The reference program's roundings to bfloat16 on the way (of `col_filtered`, `mixed_tile`, `feature`, `rebuilt` and `hammed`) count: a program that leaves them out, or rounds other values in their place, can miss the bound.
Values may be sent and summed in bfloat16 or wider, within the bound.
No kernel may reach another device: no remote copies, remote signals or barrier semaphores. Data moves between devices by JAX's collectives and lax.ppermute only.
A program may use at most 64 MiB of HBM per device.

```python
import math
import jax
import jax.numpy as jnp
from jax import lax

C = 512
R = 64
KS = 21
STEPS = 3
H = 512
W = 1024


def draw_band_input(key, part):
    key_noise, key_phase = jax.random.split(key, 2)
    vertical = (jnp.arange(H, dtype=jnp.float32) / H)[:, None, None]
    horizontal = (jnp.arange(W, dtype=jnp.float32) / W)[None, :, None]
    phases = jax.random.uniform(key_phase, (C,), jnp.float32, 0.0, 6.2831853)[None, None, :]
    smooth = 0.6 * jnp.cos(phases + 6.2831853 * (2.0 * horizontal + vertical))
    jitter = jax.random.truncated_normal(key_noise, -4.0, 4.0, (H, W, C), jnp.float32)
    amplitude = 1.0 + vertical + horizontal
    return (amplitude * (jitter + smooth)).astype(jnp.bfloat16)


def scatter_about(key, shape, width, most, kind=jnp.bfloat16):
    result = jax.random.normal(key, shape, jnp.float32) * width
    return jnp.minimum(jnp.maximum(result, -most), most).astype(kind)


def setup_inputs(seed: int = 0) -> dict:
    streams_of = jax.random.split(jax.random.key(seed), 8)
    return {
        "band_input": draw_band_input(jax.random.fold_in(streams_of[7], 71), 0),
        "column_taps": scatter_about(streams_of[1], (KS, C), 0.2, 1.0, jnp.float32),
        "row_taps": scatter_about(streams_of[2], (KS, C), 0.2, 1.0, jnp.float32),
        "w_squeeze": scatter_about(streams_of[3], (C, C), C ** -0.5, 0.25),
        "bases_init": jnp.clip(jnp.exp(jax.random.uniform(streams_of[4], (C, R), jnp.float32, math.log(0.004), math.log(0.12))), 0.004, 0.12),
        "w_ham": scatter_about(streams_of[5], (C, C), C ** -0.5, 0.25),
        "w_align": scatter_about(streams_of[6], (C, C), C ** -0.5, 0.25),
    }


EPS = 1e-6


def update_coeffs(feature, basis_now, coeffs):
    numerator = jnp.dot(feature, basis_now.astype(jnp.bfloat16), preferred_element_type=jnp.float32)
    gram_local = jnp.dot(basis_now.T, basis_now, precision=lax.Precision.HIGHEST)
    denominator = jnp.dot(coeffs, gram_local, precision=lax.Precision.HIGHEST)
    return coeffs * numerator / (denominator + EPS)


def reference(band_input, column_taps, row_taps, w_squeeze, bases_init, w_ham, w_align):
    margin = KS // 2
    padded = jnp.pad(band_input, ((0, 0), (margin, margin), (0, 0)))
    summed = jnp.zeros((H, W, C), jnp.float32)
    for offset in range(KS):
        summed = summed + column_taps[offset] * padded[:, offset:offset + W, :].astype(jnp.float32)
    col_filtered = summed.astype(jnp.bfloat16)
    padded = jnp.pad(col_filtered, ((margin, margin), (0, 0), (0, 0)))
    strip_sum = jnp.zeros((H, W, C), jnp.float32)
    for offset in range(KS):
        strip_sum = strip_sum + row_taps[offset] * padded[offset:offset + H].astype(jnp.float32)
    mixed_tile = (band_input.astype(jnp.float32) + strip_sum).astype(jnp.bfloat16).reshape(H * W, C)
    feature = jax.nn.relu(jnp.dot(mixed_tile, w_squeeze, preferred_element_type=jnp.float32)).astype(jnp.bfloat16)
    basis_now = bases_init
    scores = jnp.dot(feature, basis_now.astype(jnp.bfloat16), preferred_element_type=jnp.float32)
    coeffs = jax.nn.softmax(scores, axis=-1)
    for iteration in range(STEPS):
        coeffs = update_coeffs(feature, basis_now, coeffs)
        numerator = jnp.dot(feature.T, coeffs.astype(jnp.bfloat16), preferred_element_type=jnp.float32)
        gram_sum = jnp.dot(coeffs.T, coeffs, precision=lax.Precision.HIGHEST)
        basis_now = basis_now * numerator / (jnp.dot(basis_now, gram_sum, precision=lax.Precision.HIGHEST) + EPS)
    coeffs = update_coeffs(feature, basis_now, coeffs)
    rebuilt = jnp.dot(coeffs.astype(jnp.bfloat16), basis_now.astype(jnp.bfloat16).T, preferred_element_type=jnp.float32).astype(jnp.bfloat16)
    ham_term = jnp.dot(rebuilt, w_ham, preferred_element_type=jnp.float32)
    hammed = jax.nn.relu(feature.astype(jnp.float32) + ham_term).astype(jnp.bfloat16)
    head_out = jnp.dot(hammed, w_align, preferred_element_type=jnp.float32).astype(jnp.bfloat16)
    return head_out.reshape(H, W, C)
```

```python
import jax
import jax.numpy as jnp
from jax import lax
from jax.experimental import pallas as pl
from jax.experimental.pallas import tpu as pltpu
from jax.sharding import Mesh
from jax.sharding import PartitionSpec as P

STEPS = 3
Y, CORE, Z, X = 4, 2, 8, 4
ROWS = ("y", "core")
COLS = ("z", "x")
ALL = ("y", "core", "z", "x")
EPS = 1e-06
BF = jnp.bfloat16
F32 = jnp.float32


def padded(x, sides, width, wrap):
    for axis, dim in sides:
        count, length = (lax.axis_size(axis), x.shape[dim])
        up = [(i, (i + 1) % count) for i in range(count if wrap else count - 1)]
        down = [(j, i) for i, j in up]
        last = lax.slice_in_dim(x, length - width, length, axis=dim)
        initial = lax.slice_in_dim(x, 0, width, axis=dim)
        before = lax.ppermute(last, axis, up)
        after = lax.ppermute(initial, axis, down)
        x = jnp.concatenate([before, x, after], axis=dim)
    return x


def filter_columns(widened, column_taps, extent):
    summed = jnp.zeros((widened.shape[0], extent, widened.shape[2]), jnp.float32)
    for offset in range(column_taps.shape[0]):
        summed = summed + column_taps[offset] * widened[:, offset : offset + extent, :].astype(
            jnp.float32
        )
    return summed


def filter_rows(extended, row_taps, extent):
    summed = jnp.zeros((extent, extended.shape[1], extended.shape[2]), jnp.float32)
    for offset in range(row_taps.shape[0]):
        summed = summed + row_taps[offset] * extended[offset : offset + extent].astype(jnp.float32)
    return summed


def pair_4a(i):
    return i ^ 1


def pair_4b(i):
    return 3 - i


def pair_8a(i):
    return i ^ 1


def pair_8b(i):
    return (i + 1) % 8 if i % 2 else (i - 1) % 8


def pair_8c(i):
    return (3, 6, 5, 0, 7, 2, 1, 4)[i]


X_ROUNDS = [("x", pair_4a), ("x", pair_4b)]
Y_ROUNDS = [("y", pair_4a), ("y", pair_4b)]
Z_ROUNDS = [("z", pair_8a), ("z", pair_8b)]
LAST = [("z", pair_8c)]
ROUNDS = list(
    zip(
        X_ROUNDS + Z_ROUNDS + Y_ROUNDS + LAST,
        Z_ROUNDS + Y_ROUNDS + X_ROUNDS + LAST,
        strict=True,
    )
)


def round_pairs(by_core):
    pairs = []
    for y in range(Y):
        for c in range(CORE):
            for z in range(Z):
                for x in range(X):
                    at = {"y": y, "core": c, "z": z, "x": x}
                    axis, rule = by_core[c]
                    to = dict(at)
                    to[axis] = rule(at[axis])

                    def flat(p):
                        return ((p["y"] * CORE + p["core"]) * Z + p["z"]) * X + p["x"]

                    pairs.append((flat(at), flat(to)))
    return pairs


def summed_over_all(mine, theirs):
    swap = [(0, 1), (1, 0)]
    total = mine + lax.ppermute(theirs, "core", swap).astype(F32)
    for by_core in ROUNDS:
        got = lax.ppermute(total.astype(BF), ALL, round_pairs(by_core))
        total = total + got.astype(F32)
    return total, lax.ppermute(total, "core", swap)


def split3(a):
    hi = a.astype(BF)
    return hi, (a - hi.astype(F32)).astype(BF)


def dot(a, b, dims):
    return lax.dot_general(a, b, (dims, ((), ())), preferred_element_type=F32)


def dot3(a, b, dims):
    ah, al = split3(a)
    bh, bl = split3(b)
    return dot(ah, bh, dims) + (dot(ah, bl, dims) + dot(al, bh, dims))


NN = ((1,), (0,))
NT = ((1,), (1,))
TN = ((0,), (0,))


def coeffs_of(basis, coeffs, numerator):
    gram = dot3(basis, basis, NT)
    return coeffs * numerator / (dot3(gram, coeffs, NN) + EPS)


def emit_sums(core, coeffs, feature, mine_ref, theirs_ref):
    num = dot(coeffs.astype(BF), feature, NN)
    gram = dot3(coeffs, coeffs, NT)
    half = num.shape[0] // 2
    c = num.shape[1]
    mine_num = jnp.where(core == 0, num[:half], num[half:])
    theirs_num = jnp.where(core == 0, num[half:], num[:half])
    mine_gram = jnp.where(core == 0, gram[:half], gram[half:])
    theirs_gram = jnp.where(core == 0, gram[half:], gram[:half])
    pad = jnp.zeros((half, mine_ref.shape[1] - c - gram.shape[1]), F32)
    mine_ref[:, :c] = mine_num
    mine_ref[:, c:] = jnp.concatenate([mine_gram, pad], axis=1)
    theirs_ref[:, :c] = theirs_num.astype(BF)
    theirs_ref[:, c:] = jnp.concatenate([theirs_gram, pad], axis=1).astype(BF)


def first_kernel(core_ref, mixed_ref, w_ref, basis_ref, feature_ref, coeffs_ref, mine_ref, theirs_ref):
    feature = jnp.maximum(dot(mixed_ref[...], w_ref[...], NN), 0.0).astype(BF)
    feature_ref[...] = feature
    basis = basis_ref[...]
    scores = dot(basis.astype(BF), feature, NT)
    e = jnp.exp(scores - jnp.max(scores, axis=0, keepdims=True))
    soft = e / jnp.sum(e, axis=0, keepdims=True)
    coeffs = coeffs_of(basis, soft, scores)
    coeffs_ref[...] = coeffs
    emit_sums(core_ref[0], coeffs, feature, mine_ref, theirs_ref)


def updated_basis(core, mine_ref, other_ref, basis):
    mine, other = mine_ref[...], other_ref[...]
    both = jnp.concatenate(
        [jnp.where(core == 0, mine, other), jnp.where(core == 0, other, mine)], axis=0
    )
    r, c = basis.shape
    gram = both[:, c : c + r]
    return basis * both[:, :c] / (dot3(gram, basis, TN) + EPS)


def step_kernel(
    core_ref, smine_ref, sother_ref, basis_ref, feature_ref, coeffs_ref,
    newbasis_ref, newcoeffs_ref, mine_ref, theirs_ref,
):
    basis = updated_basis(core_ref[0], smine_ref, sother_ref, basis_ref[...])
    newbasis_ref[...] = basis
    feature = feature_ref[...]
    coeffs = coeffs_of(basis, coeffs_ref[...], dot(basis.astype(BF), feature, NT))
    newcoeffs_ref[...] = coeffs
    emit_sums(core_ref[0], coeffs, feature, mine_ref, theirs_ref)


def last_kernel(
    core_ref, smine_ref, sother_ref, basis_ref, feature_ref, coeffs_ref, wham_ref, walign_ref, out_ref
):
    basis = updated_basis(core_ref[0], smine_ref, sother_ref, basis_ref[...])
    feature = feature_ref[...]
    low = basis.astype(BF)
    coeffs = coeffs_of(basis, coeffs_ref[...], dot(low, feature, NT))
    rebuilt = dot(coeffs.astype(BF), low, TN).astype(BF)
    hammed = jnp.maximum(feature.astype(F32) + dot(rebuilt, wham_ref[...], NN), 0.0).astype(BF)
    out_ref[...] = dot(hammed, walign_ref[...], NN).astype(BF)


def call(kernel, outs, *args):
    specs = [pl.BlockSpec(memory_space=pltpu.SMEM)]
    specs += [pl.BlockSpec(memory_space=pltpu.VMEM)] * (len(args) - 1)
    return pl.pallas_call(
        kernel,
        out_shape=outs,
        in_specs=specs,
        out_specs=jax.tree.map(lambda _: pl.BlockSpec(memory_space=pltpu.VMEM), outs),
        compiler_params=pltpu.CompilerParams(vmem_limit_bytes=56 * 2**20),
    )(*args)


def on_device(band_input, column_taps, row_taps, w_squeeze, bases_init, w_ham, w_align):
    tile_rows, tile_cols, channels = band_input.shape
    margin = column_taps.shape[0] // 2
    core = lax.axis_index("core").astype(jnp.int32).reshape(1)
    framed = padded(band_input, ((ROWS, 0), (COLS, 1)), margin, False)
    col_filtered = filter_columns(framed, column_taps, tile_cols).astype(jnp.bfloat16)
    strip_sum = filter_rows(col_filtered, row_taps, tile_rows)
    mixed_tile = (
        (band_input.astype(jnp.float32) + strip_sum)
        .astype(jnp.bfloat16)
        .reshape(tile_rows * tile_cols, channels)
    )
    n, r = tile_rows * tile_cols, bases_init.shape[1]
    width = channels + 128
    sds = jax.ShapeDtypeStruct
    sums = [sds((r // 2, width), F32), sds((r // 2, width), BF)]
    basis = bases_init.T
    feature, coeffs, mine, theirs = call(
        first_kernel,
        [sds((n, channels), BF), sds((r, n), F32)] + sums,
        core, mixed_tile, w_squeeze, basis,
    )
    for _ in range(STEPS - 1):
        smine, sother = summed_over_all(mine, theirs)
        basis, coeffs, mine, theirs = call(
            step_kernel,
            [sds((r, channels), F32), sds((r, n), F32)] + sums,
            core, smine, sother, basis, feature, coeffs,
        )
    smine, sother = summed_over_all(mine, theirs)
    head_out = call(
        last_kernel,
        sds((n, channels), BF),
        core, smine, sother, basis, feature, coeffs, w_ham, w_align,
    )
    return head_out.reshape(tile_rows, tile_cols, channels)


def solution(mesh):
    split = Mesh(mesh.devices.reshape(Y, CORE, Z, X), ALL)
    in_specs = (P(ROWS, COLS, None), P(), P(), P(), P(), P(), P())
    out_specs = P(ROWS, COLS, None)
    return jax.shard_map(
        on_device, mesh=split, in_specs=in_specs, out_specs=out_specs, check_vma=False
    )
```

```python
import jax
import jax.numpy as jnp
from jax import lax
from jax.experimental import pallas as pl
from jax.experimental.pallas import tpu as pltpu
from jax.sharding import Mesh
from jax.sharding import PartitionSpec as P

STEPS = 3
Y, CORE, Z, X = 4, 2, 8, 4
ROWS = ("y", "core")
COLS = ("z", "x")
ALL = ("y", "core", "z", "x")
EPS = 1e-06
BF = jnp.bfloat16
F32 = jnp.float32


def padded(x, sides, width, wrap):
    for axis, dim in sides:
        count, length = (lax.axis_size(axis), x.shape[dim])
        up = [(i, (i + 1) % count) for i in range(count if wrap else count - 1)]
        down = [(j, i) for i, j in up]
        last = lax.slice_in_dim(x, length - width, length, axis=dim)
        initial = lax.slice_in_dim(x, 0, width, axis=dim)
        before = lax.ppermute(last, axis, up)
        after = lax.ppermute(initial, axis, down)
        x = jnp.concatenate([before, x, after], axis=dim)
    return x


def filter_columns(widened, column_taps, extent):
    summed = jnp.zeros((widened.shape[0], extent, widened.shape[2]), jnp.float32)
    for offset in range(column_taps.shape[0]):
        summed = summed + column_taps[offset] * widened[:, offset : offset + extent, :].astype(
            jnp.float32
        )
    return summed


def filter_rows(extended, row_taps, extent):
    summed = jnp.zeros((extent, extended.shape[1], extended.shape[2]), jnp.float32)
    for offset in range(row_taps.shape[0]):
        summed = summed + row_taps[offset] * extended[offset : offset + extent].astype(jnp.float32)
    return summed


def pair_4a(i):
    return i ^ 1


def pair_4b(i):
    return 3 - i


def pair_8a(i):
    return i ^ 1


def pair_8b(i):
    return (i + 1) % 8 if i % 2 else (i - 1) % 8


def pair_8c(i):
    return (3, 6, 5, 0, 7, 2, 1, 4)[i]


ROUNDS = [
    ("x", pair_4a), ("x", pair_4b), ("y", pair_4a), ("y", pair_4b),
    ("z", pair_8a), ("z", pair_8b), ("z", pair_8c),
]


def round_pairs(axis, rule):
    pairs = []
    for y in range(Y):
        for z in range(Z):
            for x in range(X):
                at = {"y": y, "z": z, "x": x}
                to = dict(at)
                to[axis] = rule(at[axis])
                flat = [((p["y"] * CORE + 1) * Z + p["z"]) * X + p["x"] for p in (at, to)]
                pairs.append(tuple(flat))
    return pairs


def summed_over_all(part):
    total = part + lax.ppermute(part.astype(BF), "core", [(0, 1)]).astype(F32)
    for axis, rule in ROUNDS:
        total = lax.optimization_barrier(total)
        got = lax.ppermute(total.astype(BF), ALL, round_pairs(axis, rule))
        total = total + got.astype(F32)
    return total, lax.ppermute(total, "core", [(1, 0)])


def split3(a):
    hi = a.astype(BF)
    return hi, (a - hi.astype(F32)).astype(BF)


def dot(a, b, dims):
    return lax.dot_general(a, b, (dims, ((), ())), preferred_element_type=F32)


def dot3(a, b, dims):
    ah, al = split3(a)
    bh, bl = split3(b)
    return dot(ah, bh, dims) + (dot(ah, bl, dims) + dot(al, bh, dims))


NN = ((1,), (0,))
NT = ((1,), (1,))
TN = ((0,), (0,))


def coeffs_of(basis, coeffs, numerator):
    gram = dot3(basis, basis, NT)
    return coeffs * numerator / (dot3(gram, coeffs, NN) + EPS)


def emit_sums(coeffs, feature, sums_ref):
    c = feature.shape[1]
    sums_ref[:, :c] = dot(coeffs.astype(BF), feature, NN)
    gram = dot3(coeffs, coeffs, NT)
    sums_ref[:, c:] = jnp.concatenate([gram, jnp.zeros_like(gram)], axis=1)


def first_kernel(mixed_ref, w_ref, basis_ref, feature_ref, coeffs_ref, sums_ref):
    feature = jnp.maximum(dot(mixed_ref[...], w_ref[...], NN), 0.0).astype(BF)
    feature_ref[...] = feature
    basis = basis_ref[...]
    scores = dot(basis.astype(BF), feature, NT)
    e = jnp.exp(scores - jnp.max(scores, axis=0, keepdims=True))
    soft = e / jnp.sum(e, axis=0, keepdims=True)
    coeffs = coeffs_of(basis, soft, scores)
    coeffs_ref[...] = coeffs
    emit_sums(coeffs, feature, sums_ref)


def updated_basis(core_ref, own_ref, got_ref, basis):
    both = jnp.where(core_ref[0] == 1, own_ref[...], got_ref[...])
    r, c = basis.shape
    gram = both[:, c : c + r]
    return basis * both[:, :c] / (dot3(gram, basis, TN) + EPS)


def step_kernel(
    core_ref, own_ref, got_ref, basis_ref, feature_ref, coeffs_ref,
    newbasis_ref, newcoeffs_ref, sums_ref,
):
    basis = updated_basis(core_ref, own_ref, got_ref, basis_ref[...])
    newbasis_ref[...] = basis
    feature = feature_ref[...]
    coeffs = coeffs_of(basis, coeffs_ref[...], dot(basis.astype(BF), feature, NT))
    newcoeffs_ref[...] = coeffs
    emit_sums(coeffs, feature, sums_ref)


def last_kernel(
    core_ref, own_ref, got_ref, basis_ref, feature_ref, coeffs_ref, wham_ref, walign_ref, out_ref
):
    basis = updated_basis(core_ref, own_ref, got_ref, basis_ref[...])
    feature = feature_ref[...]
    low = basis.astype(BF)
    coeffs = coeffs_of(basis, coeffs_ref[...], dot(low, feature, NT))
    rebuilt = dot(coeffs.astype(BF), low, TN).astype(BF)
    hammed = jnp.maximum(feature.astype(F32) + dot(rebuilt, wham_ref[...], NN), 0.0).astype(BF)
    out_ref[...] = dot(hammed, walign_ref[...], NN).astype(BF)


def call(kernel, outs, *args):
    scalar, whole = pl.BlockSpec(memory_space=pltpu.SMEM), pl.BlockSpec(memory_space=pltpu.VMEM)
    specs = [scalar if a.dtype == jnp.int32 else whole for a in args]
    return pl.pallas_call(
        kernel,
        out_shape=outs,
        in_specs=specs,
        out_specs=jax.tree.map(lambda _: pl.BlockSpec(memory_space=pltpu.VMEM), outs),
        compiler_params=pltpu.CompilerParams(vmem_limit_bytes=24 * 2**20),
    )(*args)


def on_device(band_input, column_taps, row_taps, w_squeeze, bases_init, w_ham, w_align):
    tile_rows, tile_cols, channels = band_input.shape
    margin = column_taps.shape[0] // 2
    core = lax.axis_index("core").astype(jnp.int32).reshape(1)
    framed = padded(band_input, ((ROWS, 0), (COLS, 1)), margin, False)
    col_filtered = filter_columns(framed, column_taps, tile_cols).astype(jnp.bfloat16)
    strip_sum = filter_rows(col_filtered, row_taps, tile_rows)
    mixed_tile = (
        (band_input.astype(jnp.float32) + strip_sum)
        .astype(jnp.bfloat16)
        .reshape(tile_rows * tile_cols, channels)
    )
    n, r = tile_rows * tile_cols, bases_init.shape[1]
    sds = jax.ShapeDtypeStruct
    sums = [sds((r, channels + 128), F32)]
    basis = bases_init.T
    feature, coeffs, part = call(
        first_kernel,
        [sds((n, channels), BF), sds((r, n), F32)] + sums,
        mixed_tile, w_squeeze, basis,
    )
    for _ in range(STEPS - 1):
        own, got = summed_over_all(part)
        basis, coeffs, part = call(
            step_kernel,
            [sds((r, channels), F32), sds((r, n), F32)] + sums,
            core, own, got, basis, feature, coeffs,
        )
    own, got = summed_over_all(part)
    head_out = call(
        last_kernel,
        sds((n, channels), BF),
        core, own, got, basis, feature, coeffs, w_ham, w_align,
    )
    return head_out.reshape(tile_rows, tile_cols, channels)


def solution(mesh):
    split = Mesh(mesh.devices.reshape(Y, CORE, Z, X), ALL)
    in_specs = (P(ROWS, COLS, None), P(), P(), P(), P(), P(), P())
    out_specs = P(ROWS, COLS, None)
    return jax.shard_map(
        on_device, mesh=split, in_specs=in_specs, out_specs=out_specs, check_vma=False
    )
```

```python
import jax
import jax.numpy as jnp
from jax import lax
from jax.experimental import pallas as pl
from jax.experimental.pallas import tpu as pltpu
from jax.sharding import Mesh
from jax.sharding import PartitionSpec as P

STEPS = 3
Y, CORE, Z, X = 4, 2, 8, 4
ROWS = ("y", "core")
COLS = ("z", "x")
ALL = ("y", "core", "z", "x")
EPS = 1e-06
BF = jnp.bfloat16
F32 = jnp.float32


def padded(x, sides, width, wrap):
    for axis, dim in sides:
        count, length = (lax.axis_size(axis), x.shape[dim])
        up = [(i, (i + 1) % count) for i in range(count if wrap else count - 1)]
        down = [(j, i) for i, j in up]
        last = lax.slice_in_dim(x, length - width, length, axis=dim)
        initial = lax.slice_in_dim(x, 0, width, axis=dim)
        before = lax.ppermute(last, axis, up)
        after = lax.ppermute(initial, axis, down)
        x = jnp.concatenate([before, x, after], axis=dim)
    return x


def filter_columns(widened, column_taps, extent):
    summed = jnp.zeros((widened.shape[0], extent, widened.shape[2]), jnp.float32)
    for offset in range(column_taps.shape[0]):
        summed = summed + column_taps[offset] * widened[:, offset : offset + extent, :].astype(
            jnp.float32
        )
    return summed


def filter_rows(extended, row_taps, extent):
    summed = jnp.zeros((extent, extended.shape[1], extended.shape[2]), jnp.float32)
    for offset in range(row_taps.shape[0]):
        summed = summed + row_taps[offset] * extended[offset : offset + extent].astype(jnp.float32)
    return summed


def pair_4a(i):
    return i ^ 1


def pair_4b(i):
    return 3 - i


def pair_8a(i):
    return i ^ 1


def pair_8b(i):
    return (i + 1) % 8 if i % 2 else (i - 1) % 8


def pair_8c(i):
    return (3, 6, 5, 0, 7, 2, 1, 4)[i]


ROUNDS = [
    ("x", pair_4a), ("x", pair_4b), ("y", pair_4a), ("y", pair_4b),
    ("z", pair_8a), ("z", pair_8b), ("z", pair_8c),
]


def round_pairs(axis, rule):
    pairs = []
    for y in range(Y):
        for core in range(CORE):
            for z in range(Z):
                for x in range(X):
                    at = {"y": y, "core": core, "z": z, "x": x}
                    to = dict(at, core=1 - core)
                    to[axis] = rule(at[axis])
                    pairs.append(
                        tuple(((p["y"] * CORE + p["core"]) * Z + p["z"]) * X + p["x"] for p in (at, to))
                    )
    return pairs


def summed_over_all(mine, theirs):
    swap = [(0, 1), (1, 0)]
    total = mine + lax.ppermute(theirs, "core", swap).astype(F32)
    for axis, rule in ROUNDS:
        total = lax.optimization_barrier(total)
        got = lax.ppermute(total.astype(BF), ALL, round_pairs(axis, rule))
        total = total + got.astype(F32)
    return total, lax.ppermute(total, "core", swap)


def split3(a):
    hi = a.astype(BF)
    return hi, (a - hi.astype(F32)).astype(BF)


def dot(a, b, dims):
    return lax.dot_general(a, b, (dims, ((), ())), preferred_element_type=F32)


def dot3(a, b, dims):
    ah, al = split3(a)
    bh, bl = split3(b)
    return dot(ah, bh, dims) + (dot(ah, bl, dims) + dot(al, bh, dims))


NN = ((1,), (0,))
NT = ((1,), (1,))
TN = ((0,), (0,))


def coeffs_of(basis, coeffs, numerator):
    gram = dot3(basis, basis, NT)
    return coeffs * numerator / (dot3(gram, coeffs, NN) + EPS)


def emit_sums(half_ref, coeffs, feature, mine_ref, theirs_ref):
    c, rows = feature.shape[1], mine_ref.shape[0]
    first = half_ref[0] == 0
    num = dot(coeffs.astype(BF), feature, NN)
    mine_ref[:, :c] = jnp.where(first, num[:rows], num[rows:])
    theirs_ref[:, :c] = jnp.where(first, num[rows:], num[:rows]).astype(BF)
    gram = dot3(coeffs, coeffs, NT)
    gram = jnp.concatenate([gram, jnp.zeros_like(gram)], axis=1)
    mine_ref[:, c:] = jnp.where(first, gram[:rows], gram[rows:])
    theirs_ref[:, c:] = jnp.where(first, gram[rows:], gram[:rows]).astype(BF)


def first_kernel(
    half_ref, mixed_ref, w_ref, basis_ref, feature_ref, coeffs_ref, mine_ref, theirs_ref
):
    feature = jnp.maximum(dot(mixed_ref[...], w_ref[...], NN), 0.0).astype(BF)
    feature_ref[...] = feature
    basis = basis_ref[...]
    scores = dot(basis.astype(BF), feature, NT)
    e = jnp.exp(scores - jnp.max(scores, axis=0, keepdims=True))
    soft = e / jnp.sum(e, axis=0, keepdims=True)
    coeffs = coeffs_of(basis, soft, scores)
    coeffs_ref[...] = coeffs
    emit_sums(half_ref, coeffs, feature, mine_ref, theirs_ref)


def updated_basis(half_ref, own_ref, got_ref, basis):
    own, got = own_ref[...], got_ref[...]
    first = half_ref[0] == 0
    both = jnp.concatenate([jnp.where(first, own, got), jnp.where(first, got, own)], axis=0)
    r, c = basis.shape
    gram = both[:, c : c + r]
    return basis * both[:, :c] / (dot3(gram, basis, TN) + EPS)


def step_kernel(
    half_ref, own_ref, got_ref, basis_ref, feature_ref, coeffs_ref,
    newbasis_ref, newcoeffs_ref, mine_ref, theirs_ref,
):
    basis = updated_basis(half_ref, own_ref, got_ref, basis_ref[...])
    newbasis_ref[...] = basis
    feature = feature_ref[...]
    coeffs = coeffs_of(basis, coeffs_ref[...], dot(basis.astype(BF), feature, NT))
    newcoeffs_ref[...] = coeffs
    emit_sums(half_ref, coeffs, feature, mine_ref, theirs_ref)


def last_kernel(
    half_ref, own_ref, got_ref, basis_ref, feature_ref, coeffs_ref, wham_ref, walign_ref, out_ref
):
    basis = updated_basis(half_ref, own_ref, got_ref, basis_ref[...])
    feature = feature_ref[...]
    low = basis.astype(BF)
    coeffs = coeffs_of(basis, coeffs_ref[...], dot(low, feature, NT))
    rebuilt = dot(coeffs.astype(BF), low, TN).astype(BF)
    hammed = jnp.maximum(feature.astype(F32) + dot(rebuilt, wham_ref[...], NN), 0.0).astype(BF)
    out_ref[...] = dot(hammed, walign_ref[...], NN).astype(BF)


def call(kernel, outs, *args):
    scalar, whole = pl.BlockSpec(memory_space=pltpu.SMEM), pl.BlockSpec(memory_space=pltpu.VMEM)
    specs = [scalar if a.dtype == jnp.int32 else whole for a in args]
    return pl.pallas_call(
        kernel,
        out_shape=outs,
        in_specs=specs,
        out_specs=jax.tree.map(lambda _: pl.BlockSpec(memory_space=pltpu.VMEM), outs),
        compiler_params=pltpu.CompilerParams(vmem_limit_bytes=24 * 2**20),
    )(*args)


def on_device(band_input, column_taps, row_taps, w_squeeze, bases_init, w_ham, w_align):
    tile_rows, tile_cols, channels = band_input.shape
    margin = column_taps.shape[0] // 2
    half = sum(lax.axis_index(a) for a in ALL) % 2
    half = half.astype(jnp.int32).reshape(1)
    framed = padded(band_input, ((ROWS, 0), (COLS, 1)), margin, False)
    col_filtered = filter_columns(framed, column_taps, tile_cols).astype(jnp.bfloat16)
    strip_sum = filter_rows(col_filtered, row_taps, tile_rows)
    mixed_tile = (
        (band_input.astype(jnp.float32) + strip_sum)
        .astype(jnp.bfloat16)
        .reshape(tile_rows * tile_cols, channels)
    )
    n, r = tile_rows * tile_cols, bases_init.shape[1]
    sds = jax.ShapeDtypeStruct
    width = channels + 128
    sums = [sds((r // 2, width), F32), sds((r // 2, width), BF)]
    basis = bases_init.T
    feature, coeffs, mine, theirs = call(
        first_kernel,
        [sds((n, channels), BF), sds((r, n), F32)] + sums,
        half, mixed_tile, w_squeeze, basis,
    )
    for _ in range(STEPS - 1):
        own, got = summed_over_all(mine, theirs)
        basis, coeffs, mine, theirs = call(
            step_kernel,
            [sds((r, channels), F32), sds((r, n), F32)] + sums,
            half, own, got, basis, feature, coeffs,
        )
    own, got = summed_over_all(mine, theirs)
    head_out = call(
        last_kernel,
        sds((n, channels), BF),
        half, own, got, basis, feature, coeffs, w_ham, w_align,
    )
    return head_out.reshape(tile_rows, tile_cols, channels)


def solution(mesh):
    split = Mesh(mesh.devices.reshape(Y, CORE, Z, X), ALL)
    in_specs = (P(ROWS, COLS, None), P(), P(), P(), P(), P(), P())
    out_specs = P(ROWS, COLS, None)
    return jax.shard_map(
        on_device, mesh=split, in_specs=in_specs, out_specs=out_specs, check_vma=False
    )
```

```python
import jax
import jax.numpy as jnp
from jax import lax
from jax.experimental import pallas as pl
from jax.experimental.pallas import tpu as pltpu
from jax.sharding import Mesh
from jax.sharding import PartitionSpec as P

STEPS = 3
Y, CORE, Z, X = 4, 2, 8, 4
ROWS = ("y", "core")
COLS = ("z", "x")
ALL = ("y", "core", "z", "x")
EPS = 1e-06
BF = jnp.bfloat16
F32 = jnp.float32


TAPS = 21
MARGIN = TAPS // 2
LANES = 128


def weighted(taps_ref, items, rows):
    outs = [None] * len(items)
    for k in range(TAPS):
        if not any(k in pairs for pairs in items):
            continue
        tap = jnp.broadcast_to(taps_ref[k : k + 1, :], (rows, LANES))
        for i, pairs in enumerate(items):
            if k in pairs:
                term = tap * pairs[k]
                outs[i] = term if outs[i] is None else outs[i] + term
    return outs


def own_sums(taps_ref, load, length, group, emit):
    for start in range(0, length, group):
        lo, hi = max(0, start - MARGIN), min(length, start + group + MARGIN)
        window = {i: load(i) for i in range(lo, hi)}
        items = [
            {k: window[o + k - MARGIN] for k in range(TAPS) if o + k - MARGIN in window}
            for o in range(start, start + group)
        ]
        for i, value in enumerate(weighted(taps_ref, items, 8)):
            emit(start + i, value)


def columns_own_kernel(band_ref, taps_ref, out_ref, flat, turned):
    h, w, lanes = band_ref.shape
    flat[...] = band_ref[...].astype(F32).reshape(h * w, lanes)
    for j in range(w):
        turned[j] = flat[pl.ds(j, h, stride=w), :]

    def body(i, carry):
        rows = pl.ds(pl.multiple_of(i * 8, 8), 8)

        def emit(o, value):
            out_ref[o, rows, :] = value

        own_sums(taps_ref, lambda j: turned[j, rows, :], w, 8, emit)
        return carry

    lax.fori_loop(0, h // 8, body, 0)


def columns_rest_kernel(flags_ref, own_ref, left_ref, right_ref, taps_ref, out_ref, lefts, rights, flat):
    w, h, lanes = own_ref.shape
    lefts[...] = jnp.where(flags_ref[1] == 1, left_ref[...].astype(F32), 0.0)
    rights[...] = jnp.where(flags_ref[2] == 1, right_ref[...].astype(F32), 0.0)

    def body(i, carry):
        rows = pl.ds(pl.multiple_of(i * 8, 8), 8)

        def put(o, value):
            flat[pl.ds(i * (8 * w) + o, 8, stride=w), :] = value

        before = [lefts[j, rows, :] for j in range(MARGIN)]
        items = [{j - o: before[j] for j in range(o, MARGIN)} for o in range(MARGIN)]
        for o, value in enumerate(weighted(taps_ref, items, 8)):
            put(o, own_ref[o, rows, :] + value)
        for o in range(MARGIN, w - MARGIN):
            put(o, own_ref[o, rows, :])
        after = [rights[j, rows, :] for j in range(MARGIN)]
        items = [{2 * MARGIN + j - o: after[j] for j in range(o + 1)} for o in range(MARGIN)]
        for o, value in enumerate(weighted(taps_ref, items, 8)):
            put(w - MARGIN + o, own_ref[w - MARGIN + o, rows, :] + value)
        return carry

    lax.fori_loop(0, h // 8, body, 0)
    out_ref[...] = flat[...].reshape(h, w, lanes).astype(BF)


def rows_own_kernel(filtered_ref, band_ref, taps_ref, mid_ref, top_ref, low_ref, source, residual, mixed):
    h, w, _ = filtered_ref.shape
    source[...] = filtered_ref[...].astype(F32)
    residual[...] = band_ref[...].astype(F32)

    def body(i, carry):
        cols = pl.ds(pl.multiple_of(i * 8, 8), 8)

        def emit(o, value):
            value = residual[o, cols, :] + value
            if o < MARGIN:
                top_ref[o, cols, :] = value
            elif o >= h - MARGIN:
                low_ref[o - (h - MARGIN), cols, :] = value
            else:
                mixed[o - MARGIN, cols, :] = value

        own_sums(taps_ref, lambda j: source[j, cols, :], h, 8, emit)
        return carry

    lax.fori_loop(0, w // 8, body, 0)
    mid_ref[...] = mixed[...].astype(BF)


def finished_edge(part_ref, halo_ref, taps_ref, present, pairs_of):
    blocks = []
    for start in range(0, part_ref.shape[2], LANES):
        lanes = slice(start, start + LANES)
        halo = [
            jnp.where(present, halo_ref[j, :, lanes].astype(F32), 0.0) for j in range(MARGIN)
        ]
        rows = []
        for o in range(MARGIN):
            value = part_ref[o, :, lanes]
            for k, j in pairs_of(o):
                value = value + taps_ref[k : k + 1, lanes] * halo[j]
            rows.append(value.astype(BF))
        blocks.append(jnp.concatenate(rows, axis=0))
    return jnp.concatenate(blocks, axis=1)


def pair_4a(i):
    return i ^ 1


def pair_4b(i):
    return 3 - i


def pair_8a(i):
    return i ^ 1


def pair_8b(i):
    return (i + 1) % 8 if i % 2 else (i - 1) % 8


def pair_8c(i):
    return (3, 6, 5, 0, 7, 2, 1, 4)[i]


ROUNDS = [
    ("x", pair_4a), ("x", pair_4b), ("y", pair_4a), ("y", pair_4b),
    ("z", pair_8a), ("z", pair_8b), ("z", pair_8c),
]


def round_pairs(axis, rule):
    pairs = []
    for y in range(Y):
        for core in range(CORE):
            for z in range(Z):
                for x in range(X):
                    at = {"y": y, "core": core, "z": z, "x": x}
                    to = dict(at, core=1 - core)
                    to[axis] = rule(at[axis])
                    pairs.append(
                        tuple(((p["y"] * CORE + p["core"]) * Z + p["z"]) * X + p["x"] for p in (at, to))
                    )
    return pairs


def summed_over_all(mine, theirs):
    swap = [(0, 1), (1, 0)]
    total = mine + lax.ppermute(theirs, "core", swap).astype(F32)
    for axis, rule in ROUNDS:
        total = lax.optimization_barrier(total)
        got = lax.ppermute(total.astype(BF), ALL, round_pairs(axis, rule))
        total = total + got.astype(F32)
    return total, lax.ppermute(total, "core", swap)


def split3(a):
    hi = a.astype(BF)
    return hi, (a - hi.astype(F32)).astype(BF)


def dot(a, b, dims):
    return lax.dot_general(a, b, (dims, ((), ())), preferred_element_type=F32)


def dot3(a, b, dims):
    ah, al = split3(a)
    bh, bl = split3(b)
    return dot(ah, bh, dims) + (dot(ah, bl, dims) + dot(al, bh, dims))


NN = ((1,), (0,))
NT = ((1,), (1,))
TN = ((0,), (0,))


def coeffs_of(basis, coeffs, numerator):
    gram = dot3(basis, basis, NT)
    return coeffs * numerator / (dot3(gram, coeffs, NN) + EPS)


def emit_sums(half_ref, coeffs, feature, mine_ref, theirs_ref):
    c, rows = feature.shape[1], mine_ref.shape[0]
    first = half_ref[0] == 0
    num = dot(coeffs.astype(BF), feature, NN)
    mine_ref[:, :c] = jnp.where(first, num[:rows], num[rows:])
    theirs_ref[:, :c] = jnp.where(first, num[rows:], num[:rows]).astype(BF)
    gram = dot3(coeffs, coeffs, NT)
    gram = jnp.concatenate([gram, jnp.zeros_like(gram)], axis=1)
    mine_ref[:, c:] = jnp.where(first, gram[:rows], gram[rows:])
    theirs_ref[:, c:] = jnp.where(first, gram[rows:], gram[:rows]).astype(BF)


def first_kernel(
    flags_ref, mid_ref, top_ref, low_ref, above_ref, below_ref, taps_ref, w_ref, basis_ref,
    feature_ref, coeffs_ref, mine_ref, theirs_ref,
):
    rows, cols, channels = mid_ref.shape
    edge, mid = MARGIN * cols, rows * cols
    w = w_ref[...]
    top = finished_edge(
        top_ref, above_ref, taps_ref, flags_ref[3] == 1, lambda o: [(j - o, j) for j in range(o, MARGIN)]
    )
    low = finished_edge(
        low_ref, below_ref, taps_ref, flags_ref[4] == 1, lambda o: [(2 * MARGIN + j - o, j) for j in range(o + 1)]
    )

    def squeezed(mixed):
        return jnp.maximum(dot(mixed, w, NN), 0.0).astype(BF)

    feature_ref[:edge] = squeezed(top)
    feature_ref[edge : edge + mid] = squeezed(mid_ref[...].reshape(mid, channels))
    feature_ref[edge + mid :] = squeezed(low)
    feature = feature_ref[...]
    basis = basis_ref[...]
    scores = dot(basis.astype(BF), feature, NT)
    e = jnp.exp(scores - jnp.max(scores, axis=0, keepdims=True))
    soft = e / jnp.sum(e, axis=0, keepdims=True)
    coeffs = coeffs_of(basis, soft, scores)
    coeffs_ref[...] = coeffs
    emit_sums(flags_ref, coeffs, feature, mine_ref, theirs_ref)


def updated_basis(half_ref, own_ref, got_ref, basis):
    own, got = own_ref[...], got_ref[...]
    first = half_ref[0] == 0
    both = jnp.concatenate([jnp.where(first, own, got), jnp.where(first, got, own)], axis=0)
    r, c = basis.shape
    gram = both[:, c : c + r]
    return basis * both[:, :c] / (dot3(gram, basis, TN) + EPS)


def step_kernel(
    half_ref, own_ref, got_ref, basis_ref, feature_ref, coeffs_ref,
    newbasis_ref, newcoeffs_ref, mine_ref, theirs_ref,
):
    basis = updated_basis(half_ref, own_ref, got_ref, basis_ref[...])
    newbasis_ref[...] = basis
    feature = feature_ref[...]
    coeffs = coeffs_of(basis, coeffs_ref[...], dot(basis.astype(BF), feature, NT))
    newcoeffs_ref[...] = coeffs
    emit_sums(half_ref, coeffs, feature, mine_ref, theirs_ref)


def last_kernel(
    half_ref, own_ref, got_ref, basis_ref, feature_ref, coeffs_ref, wham_ref, walign_ref, out_ref
):
    basis = updated_basis(half_ref, own_ref, got_ref, basis_ref[...])
    feature = feature_ref[...]
    low = basis.astype(BF)
    coeffs = coeffs_of(basis, coeffs_ref[...], dot(low, feature, NT))
    rebuilt = dot(coeffs.astype(BF), low, TN).astype(BF)
    hammed = jnp.maximum(feature.astype(F32) + dot(rebuilt, wham_ref[...], NN), 0.0).astype(BF)
    out_ref[...] = dot(hammed, walign_ref[...], NN).astype(BF)


def call(kernel, outs, *args):
    scalar, whole = pl.BlockSpec(memory_space=pltpu.SMEM), pl.BlockSpec(memory_space=pltpu.VMEM)
    specs = [scalar if a.dtype == jnp.int32 else whole for a in args]
    return pl.pallas_call(
        kernel,
        out_shape=outs,
        in_specs=specs,
        out_specs=jax.tree.map(lambda _: pl.BlockSpec(memory_space=pltpu.VMEM), outs),
        compiler_params=pltpu.CompilerParams(vmem_limit_bytes=24 * 2**20),
    )(*args)


def on_device(band_input, column_taps, row_taps, w_squeeze, bases_init, w_ham, w_align):
    tile_rows, tile_cols, channels = band_input.shape
    margin = column_taps.shape[0] // 2
    index = {name: lax.axis_index(name) for name in ALL}
    half = sum(index.values()) % 2
    row, col = lax.axis_index(ROWS), lax.axis_index(COLS)
    flags = [half, col > 0, col < Z * X - 1, row > 0, row < Y * CORE - 1]
    flags = jnp.stack([f.astype(jnp.int32) for f in flags])
    sds = jax.ShapeDtypeStruct

    def ring(count, by):
        return [(i, (i + by) % count) for i in range(count)]

    left = band_input[:, tile_cols - margin :].transpose(1, 0, 2)
    right = band_input[:, :margin].transpose(1, 0, 2)
    left = lax.ppermute(left, COLS, ring(Z * X, 1))
    right = lax.ppermute(right, COLS, ring(Z * X, -1))

    def blocks(*dims):
        return pl.BlockSpec((*dims, LANES), lambda i: (*(0 for _ in dims), i))

    scalar = pl.BlockSpec(memory_space=pltpu.SMEM)
    tile, turned = blocks(tile_rows, tile_cols), blocks(tile_cols, tile_rows)
    side, edge = blocks(margin, tile_rows), blocks(margin, tile_cols)
    taps = blocks(TAPS)
    grid = (channels // LANES,)
    flat = pltpu.VMEM((tile_rows * tile_cols, LANES), F32)
    params = pltpu.CompilerParams(vmem_limit_bytes=20 * 2**20)
    pixels = tile_rows * tile_cols * channels
    cost = pl.CostEstimate(flops=2 * TAPS * pixels, bytes_accessed=6 * pixels, transcendentals=0)
    own = pl.pallas_call(
        columns_own_kernel,
        grid=grid,
        in_specs=[tile, taps],
        out_specs=turned,
        out_shape=sds((tile_cols, tile_rows, channels), F32),
        scratch_shapes=[flat, pltpu.VMEM((tile_cols, tile_rows, LANES), F32)],
        compiler_params=params,
        cost_estimate=cost,
    )(band_input, column_taps)
    filtered = pl.pallas_call(
        columns_rest_kernel,
        grid=grid,
        in_specs=[scalar, turned, side, side, taps],
        out_specs=tile,
        out_shape=sds(band_input.shape, BF),
        scratch_shapes=[pltpu.VMEM((margin, tile_rows, LANES), F32)] * 2 + [flat],
        compiler_params=params,
    )(flags, own, left, right, column_taps)
    above = lax.ppermute(filtered[tile_rows - margin :], ROWS, ring(Y * CORE, 1))
    below = lax.ppermute(filtered[:margin], ROWS, ring(Y * CORE, -1))
    rest = tile_rows - 2 * margin
    mid, top, low = pl.pallas_call(
        rows_own_kernel,
        grid=grid,
        in_specs=[tile, tile, taps],
        out_specs=[blocks(rest, tile_cols), edge, edge],
        out_shape=[
            sds((rest, tile_cols, channels), BF),
            sds((margin, tile_cols, channels), F32),
            sds((margin, tile_cols, channels), F32),
        ],
        scratch_shapes=[
            pltpu.VMEM((tile_rows, tile_cols, LANES), F32),
            pltpu.VMEM((tile_rows, tile_cols, LANES), F32),
            pltpu.VMEM((rest, tile_cols, LANES), F32),
        ],
        compiler_params=params,
        cost_estimate=cost,
    )(filtered, band_input, row_taps)
    n, r = tile_rows * tile_cols, bases_init.shape[1]
    width = channels + 128
    sums = [sds((r // 2, width), F32), sds((r // 2, width), BF)]
    basis = bases_init.T
    feature, coeffs, mine, theirs = call(
        first_kernel,
        [sds((n, channels), BF), sds((r, n), F32)] + sums,
        flags, mid, top, low, above, below, row_taps, w_squeeze, basis,
    )
    for _ in range(STEPS - 1):
        own, got = summed_over_all(mine, theirs)
        basis, coeffs, mine, theirs = call(
            step_kernel,
            [sds((r, channels), F32), sds((r, n), F32)] + sums,
            flags, own, got, basis, feature, coeffs,
        )
    own, got = summed_over_all(mine, theirs)
    head_out = call(
        last_kernel,
        sds((n, channels), BF),
        flags, own, got, basis, feature, coeffs, w_ham, w_align,
    )
    return head_out.reshape(tile_rows, tile_cols, channels)


def solution(mesh):
    split = Mesh(mesh.devices.reshape(Y, CORE, Z, X), ALL)
    in_specs = (P(ROWS, COLS, None), P(), P(), P(), P(), P(), P())
    out_specs = P(ROWS, COLS, None)
    return jax.shard_map(
        on_device, mesh=split, in_specs=in_specs, out_specs=out_specs, check_vma=False
    )
```

```python
import jax
import jax.numpy as jnp
from jax import lax
from jax.experimental import pallas as pl
from jax.experimental.pallas import tpu as pltpu
from jax.sharding import Mesh
from jax.sharding import PartitionSpec as P

STEPS = 3
Y, CORE, Z, X = 4, 2, 8, 4
ROWS = ("y", "core")
COLS = ("z", "x")
ALL = ("y", "core", "z", "x")
EPS = 1e-06
BF = jnp.bfloat16
F32 = jnp.float32


TAPS = 21
MARGIN = TAPS // 2
LANES = 128
PARTS = 2


def weighted(taps_ref, items, rows):
    outs = [None] * len(items)
    for k in range(TAPS):
        if not any(k in pairs for pairs in items):
            continue
        tap = jnp.broadcast_to(taps_ref[k : k + 1, :], (rows, LANES))
        for i, pairs in enumerate(items):
            if k in pairs:
                term = tap * pairs[k]
                outs[i] = term if outs[i] is None else outs[i] + term
    return outs


def own_sums(taps_ref, load, length, group, emit):
    for start in range(0, length, group):
        lo, hi = max(0, start - MARGIN), min(length, start + group + MARGIN)
        window = {i: load(i) for i in range(lo, hi)}
        items = [
            {k: window[o + k - MARGIN] for k in range(TAPS) if o + k - MARGIN in window}
            for o in range(start, start + group)
        ]
        for i, value in enumerate(weighted(taps_ref, items, 8)):
            emit(start + i, value)


def pack_kernel(band_ref, first_ref, last_ref, flat):
    h, w, lanes = band_ref.shape
    flat[...] = band_ref[...].astype(F32).reshape(h * w, lanes)
    for j in range(MARGIN):
        first_ref[j] = flat[pl.ds(j, h, stride=w), :].astype(BF)
        last_ref[j] = flat[pl.ds(w - MARGIN + j, h, stride=w), :].astype(BF)


def columns_own_kernel(band_ref, taps_ref, out_ref, flat, turned):
    h, w, lanes = band_ref.shape
    flat[...] = band_ref[...].astype(F32).reshape(h * w, lanes)
    for j in range(w):
        turned[j] = flat[pl.ds(j, h, stride=w), :]

    def body(i, carry):
        rows = pl.ds(pl.multiple_of(i * 8, 8), 8)

        def emit(o, value):
            out_ref[o, rows, :] = value

        own_sums(taps_ref, lambda j: turned[j, rows, :], w, 8, emit)
        return carry

    lax.fori_loop(0, h // 8, body, 0)


def columns_rest_kernel(flags_ref, own_ref, left_ref, right_ref, taps_ref, out_ref, lefts, rights, flat):
    w, h, lanes = own_ref.shape
    lefts[...] = jnp.where(flags_ref[1] == 1, left_ref[...].astype(F32), 0.0)
    rights[...] = jnp.where(flags_ref[2] == 1, right_ref[...].astype(F32), 0.0)

    def body(i, carry):
        rows = pl.ds(pl.multiple_of(i * 8, 8), 8)

        def put(o, value):
            flat[pl.ds(i * (8 * w) + o, 8, stride=w), :] = value

        before = [lefts[j, rows, :] for j in range(MARGIN)]
        items = [{j - o: before[j] for j in range(o, MARGIN)} for o in range(MARGIN)]
        for o, value in enumerate(weighted(taps_ref, items, 8)):
            put(o, own_ref[o, rows, :] + value)
        for o in range(MARGIN, w - MARGIN):
            put(o, own_ref[o, rows, :])
        after = [rights[j, rows, :] for j in range(MARGIN)]
        items = [{2 * MARGIN + j - o: after[j] for j in range(o + 1)} for o in range(MARGIN)]
        for o, value in enumerate(weighted(taps_ref, items, 8)):
            put(w - MARGIN + o, own_ref[w - MARGIN + o, rows, :] + value)
        return carry

    lax.fori_loop(0, h // 8, body, 0)
    out_ref[...] = flat[...].reshape(h, w, lanes).astype(BF)


def rows_own_kernel(filtered_ref, band_ref, taps_ref, mid_ref, top_ref, low_ref, source, residual, mixed):
    h, w, _ = filtered_ref.shape
    source[...] = filtered_ref[...].astype(F32)
    residual[...] = band_ref[...].astype(F32)

    def body(i, carry):
        cols = pl.ds(pl.multiple_of(i * 8, 8), 8)

        def emit(o, value):
            value = residual[o, cols, :] + value
            if o < MARGIN:
                top_ref[o, cols, :] = value
            elif o >= h - MARGIN:
                low_ref[o - (h - MARGIN), cols, :] = value
            else:
                mixed[o - MARGIN, cols, :] = value

        own_sums(taps_ref, lambda j: source[j, cols, :], h, 8, emit)
        return carry

    lax.fori_loop(0, w // 8, body, 0)
    mid_ref[...] = mixed[...].astype(BF)


def finished_edge(part_ref, halo_ref, taps_ref, start, present, pairs_of):
    blocks = []
    for at in range(0, part_ref.shape[2], LANES):
        lanes, tap_lanes = slice(at, at + LANES), slice(start + at, start + at + LANES)
        halo = [
            jnp.where(present, halo_ref[j, :, lanes].astype(F32), 0.0) for j in range(MARGIN)
        ]
        rows = []
        for o in range(MARGIN):
            value = part_ref[o, :, lanes]
            for k, j in pairs_of(o):
                value = value + taps_ref[k : k + 1, tap_lanes] * halo[j]
            rows.append(value.astype(BF))
        blocks.append(jnp.concatenate(rows, axis=0))
    return jnp.concatenate(blocks, axis=1)


def pair_4a(i):
    return i ^ 1


def pair_4b(i):
    return 3 - i


def pair_8a(i):
    return i ^ 1


def pair_8b(i):
    return (i + 1) % 8 if i % 2 else (i - 1) % 8


def pair_8c(i):
    return (3, 6, 5, 0, 7, 2, 1, 4)[i]


ROUNDS = [
    ("x", pair_4a), ("x", pair_4b), ("y", pair_4a), ("y", pair_4b),
    ("z", pair_8a), ("z", pair_8b), ("z", pair_8c),
]


def round_pairs(axis, rule):
    pairs = []
    for y in range(Y):
        for core in range(CORE):
            for z in range(Z):
                for x in range(X):
                    at = {"y": y, "core": core, "z": z, "x": x}
                    to = dict(at, core=1 - core)
                    to[axis] = rule(at[axis])
                    pairs.append(
                        tuple(((p["y"] * CORE + p["core"]) * Z + p["z"]) * X + p["x"] for p in (at, to))
                    )
    return pairs


def summed_over_all(mine, theirs):
    swap = [(0, 1), (1, 0)]
    total = mine + lax.ppermute(theirs, "core", swap).astype(F32)
    for axis, rule in ROUNDS:
        total = lax.optimization_barrier(total)
        got = lax.ppermute(total.astype(BF), ALL, round_pairs(axis, rule))
        total = total + got.astype(F32)
    return total, lax.ppermute(total, "core", swap)


def split3(a):
    hi = a.astype(BF)
    return hi, (a - hi.astype(F32)).astype(BF)


def dot(a, b, dims):
    return lax.dot_general(a, b, (dims, ((), ())), preferred_element_type=F32)


def dot3(a, b, dims):
    ah, al = split3(a)
    bh, bl = split3(b)
    return dot(ah, bh, dims) + (dot(ah, bl, dims) + dot(al, bh, dims))


NN = ((1,), (0,))
NT = ((1,), (1,))
TN = ((0,), (0,))


def coeffs_of(basis, coeffs, numerator):
    gram = dot3(basis, basis, NT)
    return coeffs * numerator / (dot3(gram, coeffs, NN) + EPS)


def emit_sums(half_ref, coeffs, feature, mine_ref, theirs_ref):
    c, rows = feature.shape[1], mine_ref.shape[0]
    first = half_ref[0] == 0
    num = dot(coeffs.astype(BF), feature, NN)
    mine_ref[:, :c] = jnp.where(first, num[:rows], num[rows:])
    theirs_ref[:, :c] = jnp.where(first, num[rows:], num[:rows]).astype(BF)
    gram = dot3(coeffs, coeffs, NT)
    gram = jnp.concatenate([gram, jnp.zeros_like(gram)], axis=1)
    mine_ref[:, c:] = jnp.where(first, gram[:rows], gram[rows:])
    theirs_ref[:, c:] = jnp.where(first, gram[rows:], gram[:rows]).astype(BF)


def above_pairs(o):
    return [(j - o, j) for j in range(o, MARGIN)]


def below_pairs(o):
    return [(2 * MARGIN + j - o, j) for j in range(o + 1)]


def first_kernel(flags_ref, *refs):
    parts = [refs[i * 5 : i * 5 + 5] for i in range(PARTS)]
    taps_ref, w_ref, basis_ref, feature_ref, coeffs_ref, mine_ref, theirs_ref = refs[PARTS * 5 :]
    rows, cols, width = parts[0][0].shape
    edge, mid = MARGIN * cols, rows * cols
    tops, mids, lows = 0.0, 0.0, 0.0
    for i, (mid_ref, top_ref, low_ref, above_ref, below_ref) in enumerate(parts):
        w = w_ref[i * width : (i + 1) * width, :]
        top = finished_edge(top_ref, above_ref, taps_ref, i * width, flags_ref[3] == 1, above_pairs)
        low = finished_edge(low_ref, below_ref, taps_ref, i * width, flags_ref[4] == 1, below_pairs)
        tops += dot(top, w, NN)
        lows += dot(low, w, NN)
        mids += dot(mid_ref[...].reshape(mid, width), w, NN)
    feature_ref[:edge] = jnp.maximum(tops, 0.0).astype(BF)
    feature_ref[edge : edge + mid] = jnp.maximum(mids, 0.0).astype(BF)
    feature_ref[edge + mid :] = jnp.maximum(lows, 0.0).astype(BF)
    feature = feature_ref[...]
    basis = basis_ref[...]
    scores = dot(basis.astype(BF), feature, NT)
    e = jnp.exp(scores - jnp.max(scores, axis=0, keepdims=True))
    soft = e / jnp.sum(e, axis=0, keepdims=True)
    coeffs = coeffs_of(basis, soft, scores)
    coeffs_ref[...] = coeffs
    emit_sums(flags_ref, coeffs, feature, mine_ref, theirs_ref)


def updated_basis(half_ref, own_ref, got_ref, basis):
    own, got = own_ref[...], got_ref[...]
    first = half_ref[0] == 0
    both = jnp.concatenate([jnp.where(first, own, got), jnp.where(first, got, own)], axis=0)
    r, c = basis.shape
    gram = both[:, c : c + r]
    return basis * both[:, :c] / (dot3(gram, basis, TN) + EPS)


def step_kernel(
    half_ref, own_ref, got_ref, basis_ref, feature_ref, coeffs_ref,
    newbasis_ref, newcoeffs_ref, mine_ref, theirs_ref,
):
    basis = updated_basis(half_ref, own_ref, got_ref, basis_ref[...])
    newbasis_ref[...] = basis
    feature = feature_ref[...]
    coeffs = coeffs_of(basis, coeffs_ref[...], dot(basis.astype(BF), feature, NT))
    newcoeffs_ref[...] = coeffs
    emit_sums(half_ref, coeffs, feature, mine_ref, theirs_ref)


def last_kernel(
    half_ref, own_ref, got_ref, basis_ref, feature_ref, coeffs_ref, wham_ref, walign_ref, out_ref
):
    basis = updated_basis(half_ref, own_ref, got_ref, basis_ref[...])
    feature = feature_ref[...]
    low = basis.astype(BF)
    coeffs = coeffs_of(basis, coeffs_ref[...], dot(low, feature, NT))
    rebuilt = dot(coeffs.astype(BF), low, TN).astype(BF)
    hammed = jnp.maximum(feature.astype(F32) + dot(rebuilt, wham_ref[...], NN), 0.0).astype(BF)
    out_ref[...] = dot(hammed, walign_ref[...], NN).astype(BF)


def call(kernel, outs, *args):
    scalar, whole = pl.BlockSpec(memory_space=pltpu.SMEM), pl.BlockSpec(memory_space=pltpu.VMEM)
    specs = [scalar if a.dtype == jnp.int32 else whole for a in args]
    return pl.pallas_call(
        kernel,
        out_shape=outs,
        in_specs=specs,
        out_specs=jax.tree.map(lambda _: pl.BlockSpec(memory_space=pltpu.VMEM), outs),
        compiler_params=pltpu.CompilerParams(vmem_limit_bytes=24 * 2**20),
    )(*args)


def on_device(band_input, column_taps, row_taps, w_squeeze, bases_init, w_ham, w_align):
    tile_rows, tile_cols, channels = band_input.shape
    margin = column_taps.shape[0] // 2
    index = {name: lax.axis_index(name) for name in ALL}
    half = sum(index.values()) % 2
    row, col = lax.axis_index(ROWS), lax.axis_index(COLS)
    flags = [half, col > 0, col < Z * X - 1, row > 0, row < Y * CORE - 1]
    flags = jnp.stack([f.astype(jnp.int32) for f in flags])
    sds = jax.ShapeDtypeStruct

    def ring(count, by):
        return [(i, (i + by) % count) for i in range(count)]

    width = channels // PARTS
    blocks_in_part = width // LANES

    def blocks(*dims, start=0):
        return pl.BlockSpec((*dims, LANES), lambda i: (*(0 for _ in dims), i + start))

    scalar = pl.BlockSpec(memory_space=pltpu.SMEM)
    turned, tile = blocks(tile_cols, tile_rows), blocks(tile_rows, tile_cols)
    side, edge = blocks(margin, tile_rows), blocks(margin, tile_cols)
    grid = (blocks_in_part,)
    flat = pltpu.VMEM((tile_rows * tile_cols, LANES), F32)
    params = pltpu.CompilerParams(vmem_limit_bytes=20 * 2**20)
    pixels = tile_rows * tile_cols * width
    rest = tile_rows - 2 * margin

    def cost(taps, moved):
        return pl.CostEstimate(flops=2 * taps * pixels, bytes_accessed=moved * pixels, transcendentals=0)

    sides = []
    for i in range(PARTS):
        first, last = pl.pallas_call(
            pack_kernel,
            grid=grid,
            in_specs=[blocks(tile_rows, tile_cols, start=i * blocks_in_part)],
            out_specs=[side, side],
            out_shape=[sds((margin, tile_rows, width), BF)] * 2,
            scratch_shapes=[flat],
            compiler_params=params,
            cost_estimate=cost(1, 3),
        )(band_input)
        sides.append(
            (lax.ppermute(last, COLS, ring(Z * X, 1)), lax.ppermute(first, COLS, ring(Z * X, -1)))
        )
    owns = []
    for i in range(PARTS):
        start = i * blocks_in_part
        owns.append(
            pl.pallas_call(
                columns_own_kernel,
                grid=grid,
                in_specs=[blocks(tile_rows, tile_cols, start=start), blocks(TAPS, start=start)],
                out_specs=turned,
                out_shape=sds((tile_cols, tile_rows, width), F32),
                scratch_shapes=[flat, pltpu.VMEM((tile_cols, tile_rows, LANES), F32)],
                compiler_params=params,
                cost_estimate=cost(TAPS, 6),
            )(band_input, column_taps)
        )
    parts = []
    for i in range(PARTS):
        start = i * blocks_in_part
        filtered = pl.pallas_call(
            columns_rest_kernel,
            grid=grid,
            in_specs=[scalar, turned, side, side, blocks(TAPS, start=start)],
            out_specs=tile,
            out_shape=sds((tile_rows, tile_cols, width), BF),
            scratch_shapes=[pltpu.VMEM((margin, tile_rows, LANES), F32)] * 2 + [flat],
            compiler_params=params,
            cost_estimate=cost(TAPS // 2, 6),
        )(flags, owns[i], *sides[i], column_taps)
        above = lax.ppermute(filtered[tile_rows - margin :], ROWS, ring(Y * CORE, 1))
        below = lax.ppermute(filtered[:margin], ROWS, ring(Y * CORE, -1))
        mid, top, low = pl.pallas_call(
            rows_own_kernel,
            grid=grid,
            in_specs=[tile, blocks(tile_rows, tile_cols, start=start), blocks(TAPS, start=start)],
            out_specs=[blocks(rest, tile_cols), edge, edge],
            out_shape=[
                sds((rest, tile_cols, width), BF),
                sds((margin, tile_cols, width), F32),
                sds((margin, tile_cols, width), F32),
            ],
            scratch_shapes=[
                pltpu.VMEM((tile_rows, tile_cols, LANES), F32),
                pltpu.VMEM((tile_rows, tile_cols, LANES), F32),
                pltpu.VMEM((rest, tile_cols, LANES), F32),
            ],
            compiler_params=params,
            cost_estimate=cost(TAPS, 6),
        )(filtered, band_input, row_taps)
        parts += [mid, top, low, above, below]
        if i + 1 < PARTS:
            owns[i + 1], parts[-4] = lax.optimization_barrier((owns[i + 1], parts[-4]))
    n, r = tile_rows * tile_cols, bases_init.shape[1]
    packed = (r // 2, channels + LANES)
    sums = [sds(packed, F32), sds(packed, BF)]
    basis = bases_init.T
    feature, coeffs, mine, theirs = call(
        first_kernel,
        [sds((n, channels), BF), sds((r, n), F32)] + sums,
        flags, *parts, row_taps, w_squeeze, basis,
    )
    for _ in range(STEPS - 1):
        own, got = summed_over_all(mine, theirs)
        basis, coeffs, mine, theirs = call(
            step_kernel,
            [sds((r, channels), F32), sds((r, n), F32)] + sums,
            flags, own, got, basis, feature, coeffs,
        )
    own, got = summed_over_all(mine, theirs)
    head_out = call(
        last_kernel,
        sds((n, channels), BF),
        flags, own, got, basis, feature, coeffs, w_ham, w_align,
    )
    return head_out.reshape(tile_rows, tile_cols, channels)


def solution(mesh):
    split = Mesh(mesh.devices.reshape(Y, CORE, Z, X), ALL)
    in_specs = (P(ROWS, COLS, None), P(), P(), P(), P(), P(), P())
    out_specs = P(ROWS, COLS, None)
    return jax.shard_map(
        on_device, mesh=split, in_specs=in_specs, out_specs=out_specs, check_vma=False
    )
```

```python
import jax
import jax.numpy as jnp
from jax import lax
from jax.experimental import pallas as pl
from jax.experimental.pallas import tpu as pltpu
from jax.sharding import Mesh
from jax.sharding import PartitionSpec as P

STEPS = 3
Y, CORE, Z, X = 4, 2, 8, 4
ROWS = ("y", "core")
COLS = ("z", "x")
ALL = ("y", "core", "z", "x")
EPS = 1e-06
BF = jnp.bfloat16
F32 = jnp.float32


TAPS = 21
MARGIN = TAPS // 2
LANES = 128
PARTS = 2


def weighted(taps_ref, items, rows):
    outs = [None] * len(items)
    for k in range(TAPS):
        if not any(k in pairs for pairs in items):
            continue
        tap = jnp.broadcast_to(taps_ref[k : k + 1, :], (rows, LANES))
        for i, pairs in enumerate(items):
            if k in pairs:
                term = tap * pairs[k]
                outs[i] = term if outs[i] is None else outs[i] + term
    return outs


def own_sums(taps_ref, load, length, group, emit):
    for start in range(0, length, group):
        lo, hi = max(0, start - MARGIN), min(length, start + group + MARGIN)
        window = {i: load(i) for i in range(lo, hi)}
        items = [
            {k: window[o + k - MARGIN] for k in range(TAPS) if o + k - MARGIN in window}
            for o in range(start, start + group)
        ]
        for i, value in enumerate(weighted(taps_ref, items, 8)):
            emit(start + i, value)


def pack_kernel(band_ref, *refs):
    first_ref, last_ref, flat = refs[-3:]
    h, w, lanes = band_ref.shape
    flat[...] = band_ref[...].astype(F32).reshape(h * w, lanes)
    for j in range(MARGIN):
        first_ref[j] = flat[pl.ds(j, h, stride=w), :].astype(BF)
        last_ref[j] = flat[pl.ds(w - MARGIN + j, h, stride=w), :].astype(BF)


def columns_own_kernel(band_ref, taps_ref, out_ref, token_ref, flat, turned):
    h, w, lanes = band_ref.shape
    token_ref[...] = jnp.zeros_like(token_ref)
    flat[...] = band_ref[...].astype(F32).reshape(h * w, lanes)
    for j in range(w):
        turned[j] = flat[pl.ds(j, h, stride=w), :]

    def body(i, carry):
        rows = pl.ds(pl.multiple_of(i * 8, 8), 8)

        def emit(o, value):
            out_ref[o, rows, :] = value

        own_sums(taps_ref, lambda j: turned[j, rows, :], w, 8, emit)
        return carry

    lax.fori_loop(0, h // 8, body, 0)


def columns_rest_kernel(flags_ref, own_ref, left_ref, right_ref, taps_ref, *refs):
    out_ref, lefts, rights, flat = refs[-4:]
    w, h, lanes = own_ref.shape
    lefts[...] = jnp.where(flags_ref[1] == 1, left_ref[...].astype(F32), 0.0)
    rights[...] = jnp.where(flags_ref[2] == 1, right_ref[...].astype(F32), 0.0)

    def body(i, carry):
        rows = pl.ds(pl.multiple_of(i * 8, 8), 8)

        def put(o, value):
            flat[pl.ds(i * (8 * w) + o, 8, stride=w), :] = value

        before = [lefts[j, rows, :] for j in range(MARGIN)]
        items = [{j - o: before[j] for j in range(o, MARGIN)} for o in range(MARGIN)]
        for o, value in enumerate(weighted(taps_ref, items, 8)):
            put(o, own_ref[o, rows, :] + value)
        for o in range(MARGIN, w - MARGIN):
            put(o, own_ref[o, rows, :])
        after = [rights[j, rows, :] for j in range(MARGIN)]
        items = [{2 * MARGIN + j - o: after[j] for j in range(o + 1)} for o in range(MARGIN)]
        for o, value in enumerate(weighted(taps_ref, items, 8)):
            put(w - MARGIN + o, own_ref[w - MARGIN + o, rows, :] + value)
        return carry

    lax.fori_loop(0, h // 8, body, 0)
    out_ref[...] = flat[...].reshape(h, w, lanes).astype(BF)


def rows_own_kernel(filtered_ref, band_ref, taps_ref, mid_ref, top_ref, low_ref, source, residual, mixed):
    h, w, _ = filtered_ref.shape
    source[...] = filtered_ref[...].astype(F32)
    residual[...] = band_ref[...].astype(F32)

    def body(i, carry):
        cols = pl.ds(pl.multiple_of(i * 8, 8), 8)

        def emit(o, value):
            value = residual[o, cols, :] + value
            if o < MARGIN:
                top_ref[o, cols, :] = value
            elif o >= h - MARGIN:
                low_ref[o - (h - MARGIN), cols, :] = value
            else:
                mixed[o - MARGIN, cols, :] = value

        own_sums(taps_ref, lambda j: source[j, cols, :], h, 8, emit)
        return carry

    lax.fori_loop(0, w // 8, body, 0)
    mid_ref[...] = mixed[...].astype(BF)


def finished_edge(part_ref, halo_ref, taps_ref, present, pairs_of):
    blocks = []
    for start in range(0, part_ref.shape[2], LANES):
        lanes = slice(start, start + LANES)
        halo = [
            jnp.where(present, halo_ref[j, :, lanes].astype(F32), 0.0) for j in range(MARGIN)
        ]
        rows = []
        for o in range(MARGIN):
            value = part_ref[o, :, lanes]
            for k, j in pairs_of(o):
                value = value + taps_ref[k : k + 1, lanes] * halo[j]
            rows.append(value.astype(BF))
        blocks.append(jnp.concatenate(rows, axis=0))
    return jnp.concatenate(blocks, axis=1)


def pair_4a(i):
    return i ^ 1


def pair_4b(i):
    return 3 - i


def pair_8a(i):
    return i ^ 1


def pair_8b(i):
    return (i + 1) % 8 if i % 2 else (i - 1) % 8


def pair_8c(i):
    return (3, 6, 5, 0, 7, 2, 1, 4)[i]


ROUNDS = [
    ("x", pair_4a), ("x", pair_4b), ("y", pair_4a), ("y", pair_4b),
    ("z", pair_8a), ("z", pair_8b), ("z", pair_8c),
]


def round_pairs(axis, rule):
    pairs = []
    for y in range(Y):
        for core in range(CORE):
            for z in range(Z):
                for x in range(X):
                    at = {"y": y, "core": core, "z": z, "x": x}
                    to = dict(at, core=1 - core)
                    to[axis] = rule(at[axis])
                    pairs.append(
                        tuple(((p["y"] * CORE + p["core"]) * Z + p["z"]) * X + p["x"] for p in (at, to))
                    )
    return pairs


def summed_over_all(mine, theirs):
    swap = [(0, 1), (1, 0)]
    total = mine + lax.ppermute(theirs, "core", swap).astype(F32)
    for axis, rule in ROUNDS:
        total = lax.optimization_barrier(total)
        got = lax.ppermute(total.astype(BF), ALL, round_pairs(axis, rule))
        total = total + got.astype(F32)
    return total, lax.ppermute(total, "core", swap)


def split3(a):
    hi = a.astype(BF)
    return hi, (a - hi.astype(F32)).astype(BF)


def dot(a, b, dims):
    return lax.dot_general(a, b, (dims, ((), ())), preferred_element_type=F32)


def dot3(a, b, dims):
    ah, al = split3(a)
    bh, bl = split3(b)
    return dot(ah, bh, dims) + (dot(ah, bl, dims) + dot(al, bh, dims))


NN = ((1,), (0,))
NT = ((1,), (1,))
TN = ((0,), (0,))


def coeffs_of(basis, coeffs, numerator):
    gram = dot3(basis, basis, NT)
    return coeffs * numerator / (dot3(gram, coeffs, NN) + EPS)


def emit_sums(half_ref, coeffs, feature, mine_ref, theirs_ref):
    c, rows = feature.shape[1], mine_ref.shape[0]
    first = half_ref[0] == 0
    num = dot(coeffs.astype(BF), feature, NN)
    mine_ref[:, :c] = jnp.where(first, num[:rows], num[rows:])
    theirs_ref[:, :c] = jnp.where(first, num[rows:], num[:rows]).astype(BF)
    gram = dot3(coeffs, coeffs, NT)
    gram = jnp.concatenate([gram, jnp.zeros_like(gram)], axis=1)
    mine_ref[:, c:] = jnp.where(first, gram[:rows], gram[rows:])
    theirs_ref[:, c:] = jnp.where(first, gram[rows:], gram[:rows]).astype(BF)


def above_pairs(o):
    return [(j - o, j) for j in range(o, MARGIN)]


def below_pairs(o):
    return [(2 * MARGIN + j - o, j) for j in range(o + 1)]


def first_kernel(
    flags_ref, mid_ref, top_ref, low_ref, above_ref, below_ref, taps_ref, w_ref, basis_ref,
    feature_ref, coeffs_ref, mine_ref, theirs_ref,
):
    rows, cols, channels = mid_ref.shape
    edge, mid = MARGIN * cols, rows * cols
    w = w_ref[...]
    top = finished_edge(
        top_ref, above_ref, taps_ref, flags_ref[3] == 1, lambda o: [(j - o, j) for j in range(o, MARGIN)]
    )
    low = finished_edge(
        low_ref, below_ref, taps_ref, flags_ref[4] == 1, lambda o: [(2 * MARGIN + j - o, j) for j in range(o + 1)]
    )

    def squeezed(mixed):
        return jnp.maximum(dot(mixed, w, NN), 0.0).astype(BF)

    feature_ref[:edge] = squeezed(top)
    feature_ref[edge : edge + mid] = squeezed(mid_ref[...].reshape(mid, channels))
    feature_ref[edge + mid :] = squeezed(low)
    feature = feature_ref[...]
    basis = basis_ref[...]
    scores = dot(basis.astype(BF), feature, NT)
    e = jnp.exp(scores - jnp.max(scores, axis=0, keepdims=True))
    soft = e / jnp.sum(e, axis=0, keepdims=True)
    coeffs = coeffs_of(basis, soft, scores)
    coeffs_ref[...] = coeffs
    emit_sums(flags_ref, coeffs, feature, mine_ref, theirs_ref)


def updated_basis(half_ref, own_ref, got_ref, basis):
    own, got = own_ref[...], got_ref[...]
    first = half_ref[0] == 0
    both = jnp.concatenate([jnp.where(first, own, got), jnp.where(first, got, own)], axis=0)
    r, c = basis.shape
    gram = both[:, c : c + r]
    return basis * both[:, :c] / (dot3(gram, basis, TN) + EPS)


def step_kernel(
    half_ref, own_ref, got_ref, basis_ref, feature_ref, coeffs_ref,
    newbasis_ref, newcoeffs_ref, mine_ref, theirs_ref,
):
    basis = updated_basis(half_ref, own_ref, got_ref, basis_ref[...])
    newbasis_ref[...] = basis
    feature = feature_ref[...]
    coeffs = coeffs_of(basis, coeffs_ref[...], dot(basis.astype(BF), feature, NT))
    newcoeffs_ref[...] = coeffs
    emit_sums(half_ref, coeffs, feature, mine_ref, theirs_ref)


def last_kernel(
    half_ref, own_ref, got_ref, basis_ref, feature_ref, coeffs_ref, wham_ref, walign_ref, out_ref
):
    basis = updated_basis(half_ref, own_ref, got_ref, basis_ref[...])
    feature = feature_ref[...]
    low = basis.astype(BF)
    coeffs = coeffs_of(basis, coeffs_ref[...], dot(low, feature, NT))
    rebuilt = dot(coeffs.astype(BF), low, TN).astype(BF)
    hammed = jnp.maximum(feature.astype(F32) + dot(rebuilt, wham_ref[...], NN), 0.0).astype(BF)
    out_ref[...] = dot(hammed, walign_ref[...], NN).astype(BF)


def call(kernel, outs, *args):
    scalar, whole = pl.BlockSpec(memory_space=pltpu.SMEM), pl.BlockSpec(memory_space=pltpu.VMEM)
    specs = [scalar if a.dtype == jnp.int32 else whole for a in args]
    return pl.pallas_call(
        kernel,
        out_shape=outs,
        in_specs=specs,
        out_specs=jax.tree.map(lambda _: pl.BlockSpec(memory_space=pltpu.VMEM), outs),
        compiler_params=pltpu.CompilerParams(vmem_limit_bytes=24 * 2**20),
    )(*args)


def on_device(band_input, column_taps, row_taps, w_squeeze, bases_init, w_ham, w_align):
    tile_rows, tile_cols, channels = band_input.shape
    margin = column_taps.shape[0] // 2
    index = {name: lax.axis_index(name) for name in ALL}
    half = sum(index.values()) % 2
    row, col = lax.axis_index(ROWS), lax.axis_index(COLS)
    flags = [half, col > 0, col < Z * X - 1, row > 0, row < Y * CORE - 1]
    flags = jnp.stack([f.astype(jnp.int32) for f in flags])
    sds = jax.ShapeDtypeStruct

    def ring(count, by):
        return [(i, (i + by) % count) for i in range(count)]

    width = channels // PARTS
    blocks_in_part = width // LANES

    def blocks(*dims, start=0):
        return pl.BlockSpec((*dims, LANES), lambda i: (*(0 for _ in dims), i + start))

    scalar = pl.BlockSpec(memory_space=pltpu.SMEM)
    turned, tile = blocks(tile_cols, tile_rows), blocks(tile_rows, tile_cols)
    side, edge = blocks(margin, tile_rows), blocks(margin, tile_cols)
    grid = (blocks_in_part,)
    flat = pltpu.VMEM((tile_rows * tile_cols, LANES), F32)
    params = pltpu.CompilerParams(vmem_limit_bytes=20 * 2**20)
    wide = pltpu.CompilerParams(vmem_limit_bytes=58 * 2**20)
    pixels = tile_rows * tile_cols * width
    rest = tile_rows - 2 * margin

    def cost(taps, moved):
        return pl.CostEstimate(flops=2 * taps * pixels, bytes_accessed=moved * pixels, transcendentals=0)

    whole = pl.BlockSpec(memory_space=pl.ANY)
    sides, owns, tokens = [], [], []
    for i in range(PARTS):
        start = i * blocks_in_part
        first, last = pl.pallas_call(
            pack_kernel,
            grid=grid,
            in_specs=[blocks(tile_rows, tile_cols, start=start)] + [whole] * i,
            out_specs=[side, side],
            out_shape=[sds((margin, tile_rows, width), BF)] * 2,
            scratch_shapes=[flat],
            compiler_params=wide,
            cost_estimate=cost(1, 3),
        )(band_input, *tokens)
        sides.append(
            (lax.ppermute(last, COLS, ring(Z * X, 1)), lax.ppermute(first, COLS, ring(Z * X, -1)))
        )
        own, token = pl.pallas_call(
            columns_own_kernel,
            grid=grid,
            in_specs=[blocks(tile_rows, tile_cols, start=start), blocks(TAPS, start=start)],
            out_specs=[turned, pl.BlockSpec((8, LANES), lambda i: (0, 0))],
            out_shape=[sds((tile_cols, tile_rows, width), F32), sds((8, LANES), F32)],
            scratch_shapes=[flat, pltpu.VMEM((tile_cols, tile_rows, LANES), F32)],
            compiler_params=params if i else wide,
            cost_estimate=cost(TAPS, 6),
        )(band_input, column_taps)
        owns.append(own)
        tokens.append(token)
    filtered = []
    for i in range(PARTS):
        start = i * blocks_in_part
        filtered = [
            pl.pallas_call(
                columns_rest_kernel,
                grid=grid,
                in_specs=[scalar, turned, side, side, blocks(TAPS, start=start)] + [whole] * len(filtered),
                out_specs=blocks(tile_rows, tile_cols, start=start),
                out_shape=sds((tile_rows, tile_cols, channels), BF),
                scratch_shapes=[pltpu.VMEM((margin, tile_rows, LANES), F32)] * 2 + [flat],
                input_output_aliases={5: 0} if filtered else {},
                compiler_params=params,
                cost_estimate=cost(TAPS // 2, 6),
            )(flags, owns[i], *sides[i], column_taps, *filtered)
        ]
    filtered = filtered[0]
    above = lax.ppermute(filtered[tile_rows - margin :], ROWS, ring(Y * CORE, 1))
    below = lax.ppermute(filtered[:margin], ROWS, ring(Y * CORE, -1))
    mid, top, low = pl.pallas_call(
        rows_own_kernel,
        grid=(channels // LANES,),
        in_specs=[tile, tile, blocks(TAPS)],
        out_specs=[blocks(rest, tile_cols), edge, edge],
        out_shape=[
            sds((rest, tile_cols, channels), BF),
            sds((margin, tile_cols, channels), F32),
            sds((margin, tile_cols, channels), F32),
        ],
        scratch_shapes=[
            pltpu.VMEM((tile_rows, tile_cols, LANES), F32),
            pltpu.VMEM((tile_rows, tile_cols, LANES), F32),
            pltpu.VMEM((rest, tile_cols, LANES), F32),
        ],
        compiler_params=params,
        cost_estimate=cost(2 * TAPS, 12),
    )(filtered, band_input, row_taps)
    n, r = tile_rows * tile_cols, bases_init.shape[1]
    packed = (r // 2, channels + LANES)
    sums = [sds(packed, F32), sds(packed, BF)]
    basis = bases_init.T
    feature, coeffs, mine, theirs = call(
        first_kernel,
        [sds((n, channels), BF), sds((r, n), F32)] + sums,
        flags, mid, top, low, above, below, row_taps, w_squeeze, basis,
    )
    for _ in range(STEPS - 1):
        own, got = summed_over_all(mine, theirs)
        basis, coeffs, mine, theirs = call(
            step_kernel,
            [sds((r, channels), F32), sds((r, n), F32)] + sums,
            flags, own, got, basis, feature, coeffs,
        )
    own, got = summed_over_all(mine, theirs)
    head_out = call(
        last_kernel,
        sds((n, channels), BF),
        flags, own, got, basis, feature, coeffs, w_ham, w_align,
    )
    return head_out.reshape(tile_rows, tile_cols, channels)


def solution(mesh):
    split = Mesh(mesh.devices.reshape(Y, CORE, Z, X), ALL)
    in_specs = (P(ROWS, COLS, None), P(), P(), P(), P(), P(), P())
    out_specs = P(ROWS, COLS, None)
    return jax.shard_map(
        on_device, mesh=split, in_specs=in_specs, out_specs=out_specs, check_vma=False
    )
```

```python
import jax
import jax.numpy as jnp
from jax import lax
from jax.experimental import pallas as pl
from jax.experimental.pallas import tpu as pltpu
from jax.sharding import Mesh
from jax.sharding import PartitionSpec as P

STEPS = 3
Y, CORE, Z, X = 4, 2, 8, 4
ROWS = ("y", "core")
COLS = ("z", "x")
ALL = ("y", "core", "z", "x")
EPS = 1e-06
BF = jnp.bfloat16
F32 = jnp.float32


TAPS = 21
MARGIN = TAPS // 2
LANES = 128
PARTS = 2
HEAD_BLOCKS = 4


def weighted(taps_ref, items, rows):
    outs = [None] * len(items)
    for k in range(TAPS):
        if not any(k in pairs for pairs in items):
            continue
        tap = jnp.broadcast_to(taps_ref[k : k + 1, :], (rows, LANES))
        for i, pairs in enumerate(items):
            if k in pairs:
                term = tap * pairs[k]
                outs[i] = term if outs[i] is None else outs[i] + term
    return outs


def own_sums(taps_ref, load, length, group, emit):
    for start in range(0, length, group):
        lo, hi = max(0, start - MARGIN), min(length, start + group + MARGIN)
        window = {i: load(i) for i in range(lo, hi)}
        items = [
            {k: window[o + k - MARGIN] for k in range(TAPS) if o + k - MARGIN in window}
            for o in range(start, start + group)
        ]
        for i, value in enumerate(weighted(taps_ref, items, 8)):
            emit(start + i, value)


def pack_kernel(band_ref, first_ref, last_ref, flat):
    h, w, lanes = band_ref.shape
    flat[...] = band_ref[...].astype(F32).reshape(h * w, lanes)
    for j in range(MARGIN):
        first_ref[j] = flat[pl.ds(j, h, stride=w), :].astype(BF)
        last_ref[j] = flat[pl.ds(w - MARGIN + j, h, stride=w), :].astype(BF)


def columns_own_kernel(band_ref, taps_ref, out_ref, flat, turned):
    h, w, lanes = band_ref.shape
    flat[...] = band_ref[...].astype(F32).reshape(h * w, lanes)
    for j in range(w):
        turned[j] = flat[pl.ds(j, h, stride=w), :]

    def body(i, carry):
        rows = pl.ds(pl.multiple_of(i * 8, 8), 8)

        def emit(o, value):
            out_ref[o, rows, :] = value

        own_sums(taps_ref, lambda j: turned[j, rows, :], w, 8, emit)
        return carry

    lax.fori_loop(0, h // 8, body, 0)


def columns_rest_kernel(flags_ref, own_ref, left_ref, right_ref, taps_ref, *refs):
    out_ref, lefts, rights, flat = refs[-4:]
    w, h, lanes = own_ref.shape
    lefts[...] = jnp.where(flags_ref[1] == 1, left_ref[...].astype(F32), 0.0)
    rights[...] = jnp.where(flags_ref[2] == 1, right_ref[...].astype(F32), 0.0)

    def body(i, carry):
        rows = pl.ds(pl.multiple_of(i * 8, 8), 8)

        def put(o, value):
            flat[pl.ds(i * (8 * w) + o, 8, stride=w), :] = value

        before = [lefts[j, rows, :] for j in range(MARGIN)]
        items = [{j - o: before[j] for j in range(o, MARGIN)} for o in range(MARGIN)]
        for o, value in enumerate(weighted(taps_ref, items, 8)):
            put(o, own_ref[o, rows, :] + value)
        for o in range(MARGIN, w - MARGIN):
            put(o, own_ref[o, rows, :])
        after = [rights[j, rows, :] for j in range(MARGIN)]
        items = [{2 * MARGIN + j - o: after[j] for j in range(o + 1)} for o in range(MARGIN)]
        for o, value in enumerate(weighted(taps_ref, items, 8)):
            put(w - MARGIN + o, own_ref[w - MARGIN + o, rows, :] + value)
        return carry

    lax.fori_loop(0, h // 8, body, 0)
    out_ref[...] = flat[...].reshape(h, w, lanes).astype(BF)


def rows_own_kernel(filtered_ref, band_ref, taps_ref, mid_ref, top_ref, low_ref, source, residual, mixed):
    h, w, _ = filtered_ref.shape
    source[...] = filtered_ref[...].astype(F32)
    residual[...] = band_ref[...].astype(F32)

    def body(i, carry):
        cols = pl.ds(pl.multiple_of(i * 8, 8), 8)

        def emit(o, value):
            value = residual[o, cols, :] + value
            if o < MARGIN:
                top_ref[o, cols, :] = value
            elif o >= h - MARGIN:
                low_ref[o - (h - MARGIN), cols, :] = value
            else:
                mixed[o - MARGIN, cols, :] = value

        own_sums(taps_ref, lambda j: source[j, cols, :], h, 8, emit)
        return carry

    lax.fori_loop(0, w // 8, body, 0)
    mid_ref[...] = mixed[...].astype(BF)


def finished_edge(part_ref, halo_ref, taps_ref, present, pairs_of):
    blocks = []
    for start in range(0, part_ref.shape[2], LANES):
        lanes = slice(start, start + LANES)
        halo = [
            jnp.where(present, halo_ref[j, :, lanes].astype(F32), 0.0) for j in range(MARGIN)
        ]
        rows = []
        for o in range(MARGIN):
            value = part_ref[o, :, lanes]
            for k, j in pairs_of(o):
                value = value + taps_ref[k : k + 1, lanes] * halo[j]
            rows.append(value.astype(BF))
        blocks.append(jnp.concatenate(rows, axis=0))
    return jnp.concatenate(blocks, axis=1)


def pair_4a(i):
    return i ^ 1


def pair_4b(i):
    return 3 - i


def pair_8a(i):
    return i ^ 1


def pair_8b(i):
    return (i + 1) % 8 if i % 2 else (i - 1) % 8


def pair_8c(i):
    return (3, 6, 5, 0, 7, 2, 1, 4)[i]


ROUNDS = [
    ("x", pair_4a), ("x", pair_4b), ("y", pair_4a), ("y", pair_4b),
    ("z", pair_8a), ("z", pair_8b), ("z", pair_8c),
]


def round_pairs(axis, rule):
    pairs = []
    for y in range(Y):
        for core in range(CORE):
            for z in range(Z):
                for x in range(X):
                    at = {"y": y, "core": core, "z": z, "x": x}
                    to = dict(at, core=1 - core)
                    to[axis] = rule(at[axis])
                    pairs.append(
                        tuple(((p["y"] * CORE + p["core"]) * Z + p["z"]) * X + p["x"] for p in (at, to))
                    )
    return pairs


def summed_over_all(mine, theirs):
    swap = [(0, 1), (1, 0)]
    total = mine + lax.ppermute(theirs, "core", swap).astype(F32)
    for axis, rule in ROUNDS:
        total = lax.optimization_barrier(total)
        got = lax.ppermute(total.astype(BF), ALL, round_pairs(axis, rule))
        total = total + got.astype(F32)
    return total, lax.ppermute(total, "core", swap)


def split3(a):
    hi = a.astype(BF)
    return hi, (a - hi.astype(F32)).astype(BF)


def dot(a, b, dims):
    return lax.dot_general(a, b, (dims, ((), ())), preferred_element_type=F32)


def dot3(a, b, dims):
    ah, al = split3(a)
    bh, bl = split3(b)
    return dot(ah, bh, dims) + (dot(ah, bl, dims) + dot(al, bh, dims))


NN = ((1,), (0,))
NT = ((1,), (1,))
TN = ((0,), (0,))


def coeffs_of(basis, coeffs, numerator):
    gram = dot3(basis, basis, NT)
    return coeffs * numerator / (dot3(gram, coeffs, NN) + EPS)


def emit_sums(half_ref, coeffs, feature, mine_ref, theirs_ref):
    c, rows = feature.shape[1], mine_ref.shape[0]
    first = half_ref[0] == 0
    num = dot(coeffs.astype(BF), feature, NN)
    mine_ref[:, :c] = jnp.where(first, num[:rows], num[rows:])
    theirs_ref[:, :c] = jnp.where(first, num[rows:], num[:rows]).astype(BF)
    gram = dot3(coeffs, coeffs, NT)
    gram = jnp.concatenate([gram, jnp.zeros_like(gram)], axis=1)
    mine_ref[:, c:] = jnp.where(first, gram[:rows], gram[rows:])
    theirs_ref[:, c:] = jnp.where(first, gram[rows:], gram[:rows]).astype(BF)


def above_pairs(o):
    return [(j - o, j) for j in range(o, MARGIN)]


def below_pairs(o):
    return [(2 * MARGIN + j - o, j) for j in range(o + 1)]


def first_kernel(
    flags_ref, mid_ref, top_ref, low_ref, above_ref, below_ref, taps_ref, w_ref, basis_ref,
    feature_ref, coeffs_ref, mine_ref, theirs_ref,
):
    rows, cols, channels = mid_ref.shape
    edge, mid = MARGIN * cols, rows * cols
    w = w_ref[...]
    top = finished_edge(
        top_ref, above_ref, taps_ref, flags_ref[3] == 1, lambda o: [(j - o, j) for j in range(o, MARGIN)]
    )
    low = finished_edge(
        low_ref, below_ref, taps_ref, flags_ref[4] == 1, lambda o: [(2 * MARGIN + j - o, j) for j in range(o + 1)]
    )

    def squeezed(mixed):
        return jnp.maximum(dot(mixed, w, NN), 0.0).astype(BF)

    feature_ref[:edge] = squeezed(top)
    feature_ref[edge : edge + mid] = squeezed(mid_ref[...].reshape(mid, channels))
    feature_ref[edge + mid :] = squeezed(low)
    feature = feature_ref[...]
    basis = basis_ref[...]
    scores = dot(basis.astype(BF), feature, NT)
    e = jnp.exp(scores - jnp.max(scores, axis=0, keepdims=True))
    soft = e / jnp.sum(e, axis=0, keepdims=True)
    coeffs = coeffs_of(basis, soft, scores)
    coeffs_ref[...] = coeffs
    emit_sums(flags_ref, coeffs, feature, mine_ref, theirs_ref)


def updated_basis(half_ref, own_ref, got_ref, basis):
    own, got = own_ref[...], got_ref[...]
    first = half_ref[0] == 0
    both = jnp.concatenate([jnp.where(first, own, got), jnp.where(first, got, own)], axis=0)
    r, c = basis.shape
    gram = both[:, c : c + r]
    return basis * both[:, :c] / (dot3(gram, basis, TN) + EPS)


def step_kernel(
    half_ref, own_ref, got_ref, basis_ref, feature_ref, coeffs_ref,
    newbasis_ref, newcoeffs_ref, mine_ref, theirs_ref,
):
    basis = updated_basis(half_ref, own_ref, got_ref, basis_ref[...])
    newbasis_ref[...] = basis
    feature = feature_ref[...]
    coeffs = coeffs_of(basis, coeffs_ref[...], dot(basis.astype(BF), feature, NT))
    newcoeffs_ref[...] = coeffs
    emit_sums(half_ref, coeffs, feature, mine_ref, theirs_ref)


def last_kernel(
    half_ref, own_ref, got_ref, basis_ref, feature_ref, coeffs_ref, wham_ref, walign_ref, out_ref, now
):
    @pl.when(pl.program_id(0) == 0)
    def _():
        now[...] = updated_basis(half_ref, own_ref, got_ref, basis_ref[...])

    basis = now[...]
    feature = feature_ref[...]
    low = basis.astype(BF)
    coeffs = coeffs_of(basis, coeffs_ref[...], dot(low, feature, NT))
    rebuilt = dot(coeffs.astype(BF), low, TN).astype(BF)
    hammed = jnp.maximum(feature.astype(F32) + dot(rebuilt, wham_ref[...], NN), 0.0).astype(BF)
    out_ref[...] = dot(hammed, walign_ref[...], NN).astype(BF)


def call(kernel, outs, *args):
    scalar, whole = pl.BlockSpec(memory_space=pltpu.SMEM), pl.BlockSpec(memory_space=pltpu.VMEM)
    specs = [scalar if a.dtype == jnp.int32 else whole for a in args]
    return pl.pallas_call(
        kernel,
        out_shape=outs,
        in_specs=specs,
        out_specs=jax.tree.map(lambda _: pl.BlockSpec(memory_space=pltpu.VMEM), outs),
        compiler_params=pltpu.CompilerParams(vmem_limit_bytes=24 * 2**20),
    )(*args)


def on_device(band_input, column_taps, row_taps, w_squeeze, bases_init, w_ham, w_align):
    tile_rows, tile_cols, channels = band_input.shape
    margin = column_taps.shape[0] // 2
    index = {name: lax.axis_index(name) for name in ALL}
    half = sum(index.values()) % 2
    row, col = lax.axis_index(ROWS), lax.axis_index(COLS)
    flags = [half, col > 0, col < Z * X - 1, row > 0, row < Y * CORE - 1]
    flags = jnp.stack([f.astype(jnp.int32) for f in flags])
    sds = jax.ShapeDtypeStruct

    def ring(count, by):
        return [(i, (i + by) % count) for i in range(count)]

    width = channels // PARTS
    blocks_in_part = width // LANES

    def blocks(*dims, start=0):
        return pl.BlockSpec((*dims, LANES), lambda i: (*(0 for _ in dims), i + start))

    scalar = pl.BlockSpec(memory_space=pltpu.SMEM)
    turned, tile = blocks(tile_cols, tile_rows), blocks(tile_rows, tile_cols)
    side, edge = blocks(margin, tile_rows), blocks(margin, tile_cols)
    grid = (blocks_in_part,)
    flat = pltpu.VMEM((tile_rows * tile_cols, LANES), F32)
    params = pltpu.CompilerParams(vmem_limit_bytes=20 * 2**20)
    wide = pltpu.CompilerParams(vmem_limit_bytes=58 * 2**20)
    pixels = tile_rows * tile_cols * width
    rest = tile_rows - 2 * margin

    def cost(taps, moved):
        return pl.CostEstimate(flops=2 * taps * pixels, bytes_accessed=moved * pixels, transcendentals=0)

    whole = pl.BlockSpec(memory_space=pl.ANY)
    sides = []
    for i in range(PARTS):
        start = i * blocks_in_part
        first, last = pl.pallas_call(
            pack_kernel,
            grid=grid,
            in_specs=[blocks(tile_rows, tile_cols, start=start)],
            out_specs=[side, side],
            out_shape=[sds((margin, tile_rows, width), BF)] * 2,
            scratch_shapes=[flat],
            compiler_params=wide if i == 0 else params,
            cost_estimate=cost(1, 3),
        )(band_input)
        sides.append(
            (lax.ppermute(last, COLS, ring(Z * X, 1)), lax.ppermute(first, COLS, ring(Z * X, -1)))
        )
    own = pl.pallas_call(
        columns_own_kernel,
        grid=(channels // LANES,),
        in_specs=[tile, blocks(TAPS)],
        out_specs=turned,
        out_shape=sds((tile_cols, tile_rows, channels), F32),
        scratch_shapes=[flat, pltpu.VMEM((tile_cols, tile_rows, LANES), F32)],
        compiler_params=params,
        cost_estimate=cost(2 * TAPS, 12),
    )(band_input, column_taps)
    filtered = []
    for i in range(PARTS):
        start = i * blocks_in_part
        filtered = [
            pl.pallas_call(
                columns_rest_kernel,
                grid=grid,
                in_specs=[scalar, blocks(tile_cols, tile_rows, start=start), side, side, blocks(TAPS, start=start)] + [whole] * len(filtered),
                out_specs=blocks(tile_rows, tile_cols, start=start),
                out_shape=sds((tile_rows, tile_cols, channels), BF),
                scratch_shapes=[pltpu.VMEM((margin, tile_rows, LANES), F32)] * 2 + [flat],
                input_output_aliases={5: 0} if filtered else {},
                compiler_params=params,
                cost_estimate=cost(TAPS // 2, 6),
            )(flags, own, *sides[i], column_taps, *filtered)
        ]
    filtered = filtered[0]
    above = lax.ppermute(filtered[tile_rows - margin :], ROWS, ring(Y * CORE, 1))
    below = lax.ppermute(filtered[:margin], ROWS, ring(Y * CORE, -1))
    mid, top, low = pl.pallas_call(
        rows_own_kernel,
        grid=(channels // LANES,),
        in_specs=[tile, tile, blocks(TAPS)],
        out_specs=[blocks(rest, tile_cols), edge, edge],
        out_shape=[
            sds((rest, tile_cols, channels), BF),
            sds((margin, tile_cols, channels), F32),
            sds((margin, tile_cols, channels), F32),
        ],
        scratch_shapes=[
            pltpu.VMEM((tile_rows, tile_cols, LANES), F32),
            pltpu.VMEM((tile_rows, tile_cols, LANES), F32),
            pltpu.VMEM((rest, tile_cols, LANES), F32),
        ],
        compiler_params=params,
        cost_estimate=cost(2 * TAPS, 12),
    )(filtered, band_input, row_taps)
    n, r = tile_rows * tile_cols, bases_init.shape[1]
    packed = (r // 2, channels + LANES)
    sums = [sds(packed, F32), sds(packed, BF)]
    basis = bases_init.T
    feature, coeffs, mine, theirs = call(
        first_kernel,
        [sds((n, channels), BF), sds((r, n), F32)] + sums,
        flags, mid, top, low, above, below, row_taps, w_squeeze, basis,
    )
    for _ in range(STEPS - 1):
        own, got = summed_over_all(mine, theirs)
        basis, coeffs, mine, theirs = call(
            step_kernel,
            [sds((r, channels), F32), sds((r, n), F32)] + sums,
            flags, own, got, basis, feature, coeffs,
        )
    own, got = summed_over_all(mine, theirs)
    vmem = pl.BlockSpec(memory_space=pltpu.VMEM)
    pixel_block = n // HEAD_BLOCKS
    pixels_by_channel = pl.BlockSpec((pixel_block, channels), lambda i: (i, 0))
    head_out = pl.pallas_call(
        last_kernel,
        grid=(HEAD_BLOCKS,),
        in_specs=[scalar, vmem, vmem, vmem, pixels_by_channel]
        + [pl.BlockSpec((r, pixel_block), lambda i: (0, i)), vmem, vmem],
        out_specs=pixels_by_channel,
        out_shape=sds((n, channels), BF),
        scratch_shapes=[pltpu.VMEM((r, channels), F32)],
        compiler_params=pltpu.CompilerParams(vmem_limit_bytes=24 * 2**20),
    )(flags, own, got, basis, feature, coeffs, w_ham, w_align)
    return head_out.reshape(tile_rows, tile_cols, channels)


def solution(mesh):
    split = Mesh(mesh.devices.reshape(Y, CORE, Z, X), ALL)
    in_specs = (P(ROWS, COLS, None), P(), P(), P(), P(), P(), P())
    out_specs = P(ROWS, COLS, None)
    return jax.shard_map(
        on_device, mesh=split, in_specs=in_specs, out_specs=out_specs, check_vma=False
    )
```

```python
import jax
import jax.numpy as jnp
from jax import lax
from jax.experimental import pallas as pl
from jax.experimental.pallas import tpu as pltpu
from jax.sharding import Mesh
from jax.sharding import PartitionSpec as P

STEPS = 3
Y, CORE, Z, X = 4, 2, 8, 4
ROWS = ("y", "core")
COLS = ("z", "x")
ALL = ("y", "core", "z", "x")
EPS = 1e-06
BF = jnp.bfloat16
F32 = jnp.float32


TAPS = 21
MARGIN = TAPS // 2
LANES = 128
PARTS = 2


def weighted(taps_ref, items, rows):
    outs = [None] * len(items)
    for k in range(TAPS):
        if not any(k in pairs for pairs in items):
            continue
        tap = jnp.broadcast_to(taps_ref[k : k + 1, :], (rows, LANES))
        for i, pairs in enumerate(items):
            if k in pairs:
                term = tap * pairs[k]
                outs[i] = term if outs[i] is None else outs[i] + term
    return outs


def own_sums(taps_ref, load, length, group, emit):
    for start in range(0, length, group):
        lo, hi = max(0, start - MARGIN), min(length, start + group + MARGIN)
        window = {i: load(i) for i in range(lo, hi)}
        items = [
            {k: window[o + k - MARGIN] for k in range(TAPS) if o + k - MARGIN in window}
            for o in range(start, start + group)
        ]
        for i, value in enumerate(weighted(taps_ref, items, 8)):
            emit(start + i, value)


def pack_kernel(band_ref, first_ref, last_ref, flat):
    h, w, lanes = band_ref.shape
    flat[...] = band_ref[...].astype(F32).reshape(h * w, lanes)
    for j in range(MARGIN):
        first_ref[j] = flat[pl.ds(j, h, stride=w), :].astype(BF)
        last_ref[j] = flat[pl.ds(w - MARGIN + j, h, stride=w), :].astype(BF)


def columns_own_kernel(band_ref, taps_ref, out_ref, flat, turned):
    h, w, lanes = band_ref.shape
    flat[...] = band_ref[...].astype(F32).reshape(h * w, lanes)
    for j in range(w):
        turned[j] = flat[pl.ds(j, h, stride=w), :]

    def body(i, carry):
        rows = pl.ds(pl.multiple_of(i * 8, 8), 8)

        def emit(o, value):
            out_ref[o, rows, :] = value

        own_sums(taps_ref, lambda j: turned[j, rows, :], w, 8, emit)
        return carry

    lax.fori_loop(0, h // 8, body, 0)


def columns_rest_kernel(flags_ref, own_ref, left_ref, right_ref, taps_ref, *refs):
    out_ref, lefts, rights, flat = refs[-4:]
    w, h, lanes = own_ref.shape
    lefts[...] = jnp.where(flags_ref[1] == 1, left_ref[...].astype(F32), 0.0)
    rights[...] = jnp.where(flags_ref[2] == 1, right_ref[...].astype(F32), 0.0)

    def body(i, carry):
        rows = pl.ds(pl.multiple_of(i * 8, 8), 8)

        def put(o, value):
            flat[pl.ds(i * (8 * w) + o, 8, stride=w), :] = value

        before = [lefts[j, rows, :] for j in range(MARGIN)]
        items = [{j - o: before[j] for j in range(o, MARGIN)} for o in range(MARGIN)]
        for o, value in enumerate(weighted(taps_ref, items, 8)):
            put(o, own_ref[o, rows, :] + value)
        for o in range(MARGIN, w - MARGIN):
            put(o, own_ref[o, rows, :])
        after = [rights[j, rows, :] for j in range(MARGIN)]
        items = [{2 * MARGIN + j - o: after[j] for j in range(o + 1)} for o in range(MARGIN)]
        for o, value in enumerate(weighted(taps_ref, items, 8)):
            put(w - MARGIN + o, own_ref[w - MARGIN + o, rows, :] + value)
        return carry

    lax.fori_loop(0, h // 8, body, 0)
    out_ref[...] = flat[...].reshape(h, w, lanes).astype(BF)


def rows_own_kernel(filtered_ref, band_ref, taps_ref, mid_ref, top_ref, low_ref, source, residual, mixed):
    h, w, _ = filtered_ref.shape
    source[...] = filtered_ref[...].astype(F32)
    residual[...] = band_ref[...].astype(F32)

    def body(i, carry):
        cols = pl.ds(pl.multiple_of(i * 8, 8), 8)

        def emit(o, value):
            value = residual[o, cols, :] + value
            if o < MARGIN:
                top_ref[o, cols, :] = value
            elif o >= h - MARGIN:
                low_ref[o - (h - MARGIN), cols, :] = value
            else:
                mixed[o - MARGIN, cols, :] = value

        own_sums(taps_ref, lambda j: source[j, cols, :], h, 8, emit)
        return carry

    lax.fori_loop(0, w // 8, body, 0)
    mid_ref[...] = mixed[...].astype(BF)


def finished_edge(part_ref, halo_ref, taps_ref, present, pairs_of):
    blocks = []
    for start in range(0, part_ref.shape[2], LANES):
        lanes = slice(start, start + LANES)
        halo = [
            jnp.where(present, halo_ref[j, :, lanes].astype(F32), 0.0) for j in range(MARGIN)
        ]
        rows = []
        for o in range(MARGIN):
            value = part_ref[o, :, lanes]
            for k, j in pairs_of(o):
                value = value + taps_ref[k : k + 1, lanes] * halo[j]
            rows.append(value.astype(BF))
        blocks.append(jnp.concatenate(rows, axis=0))
    return jnp.concatenate(blocks, axis=1)


def pair_4a(i):
    return i ^ 1


def pair_4b(i):
    return 3 - i


def pair_8a(i):
    return i ^ 1


def pair_8b(i):
    return (i + 1) % 8 if i % 2 else (i - 1) % 8


def pair_8c(i):
    return (3, 6, 5, 0, 7, 2, 1, 4)[i]


ROUNDS = [
    ("x", pair_4a), ("x", pair_4b), ("y", pair_4a), ("y", pair_4b),
    ("z", pair_8a), ("z", pair_8b), ("z", pair_8c),
]


def round_pairs(axis, rule):
    pairs = []
    for y in range(Y):
        for core in range(CORE):
            for z in range(Z):
                for x in range(X):
                    at = {"y": y, "core": core, "z": z, "x": x}
                    to = dict(at, core=1 - core)
                    to[axis] = rule(at[axis])
                    pairs.append(
                        tuple(((p["y"] * CORE + p["core"]) * Z + p["z"]) * X + p["x"] for p in (at, to))
                    )
    return pairs


def summed_over_all(mine, theirs):
    swap = [(0, 1), (1, 0)]
    total = mine + lax.ppermute(theirs, "core", swap).astype(F32)
    for axis, rule in ROUNDS:
        total = lax.optimization_barrier(total)
        got = lax.ppermute(total.astype(BF), ALL, round_pairs(axis, rule))
        total = total + got.astype(F32)
    return total, lax.ppermute(total, "core", swap)


def split3(a):
    hi = a.astype(BF)
    return hi, (a - hi.astype(F32)).astype(BF)


def dot(a, b, dims):
    return lax.dot_general(a, b, (dims, ((), ())), preferred_element_type=F32)


def dot3(a, b, dims):
    ah, al = split3(a)
    bh, bl = split3(b)
    return dot(ah, bh, dims) + (dot(ah, bl, dims) + dot(al, bh, dims))


NN = ((1,), (0,))
NT = ((1,), (1,))
TN = ((0,), (0,))


def coeffs_of(basis, coeffs, numerator):
    gram = dot3(basis, basis, NT)
    return coeffs * numerator / (dot3(coeffs, gram, NN) + EPS)


def emit_sums(half_ref, coeffs, feature, mine_ref, theirs_ref):
    c, rows = feature.shape[1], mine_ref.shape[0]
    first = half_ref[0] == 0
    num = dot(coeffs.astype(BF), feature, TN)
    mine_ref[:, :c] = jnp.where(first, num[:rows], num[rows:])
    theirs_ref[:, :c] = jnp.where(first, num[rows:], num[:rows]).astype(BF)
    gram = dot3(coeffs, coeffs, TN)
    gram = jnp.concatenate([gram, jnp.zeros_like(gram)], axis=1)
    mine_ref[:, c:] = jnp.where(first, gram[:rows], gram[rows:])
    theirs_ref[:, c:] = jnp.where(first, gram[rows:], gram[:rows]).astype(BF)


def above_pairs(o):
    return [(j - o, j) for j in range(o, MARGIN)]


def below_pairs(o):
    return [(2 * MARGIN + j - o, j) for j in range(o + 1)]


def first_kernel(
    flags_ref, mid_ref, top_ref, low_ref, above_ref, below_ref, taps_ref, w_ref, basis_ref,
    feature_ref, coeffs_ref, mine_ref, theirs_ref,
):
    rows, cols, channels = mid_ref.shape
    edge, mid = MARGIN * cols, rows * cols
    w = w_ref[...]
    top = finished_edge(
        top_ref, above_ref, taps_ref, flags_ref[3] == 1, lambda o: [(j - o, j) for j in range(o, MARGIN)]
    )
    low = finished_edge(
        low_ref, below_ref, taps_ref, flags_ref[4] == 1, lambda o: [(2 * MARGIN + j - o, j) for j in range(o + 1)]
    )

    def squeezed(mixed):
        return jnp.maximum(dot(mixed, w, NN), 0.0).astype(BF)

    feature_ref[:edge] = squeezed(top)
    feature_ref[edge : edge + mid] = squeezed(mid_ref[...].reshape(mid, channels))
    feature_ref[edge + mid :] = squeezed(low)
    feature = feature_ref[...]
    basis = basis_ref[...]
    scores = dot(feature, basis.astype(BF), NT)
    e = jnp.exp(scores - jnp.max(scores, axis=1, keepdims=True))
    soft = e / jnp.sum(e, axis=1, keepdims=True)
    coeffs = coeffs_of(basis, soft, scores)
    coeffs_ref[...] = coeffs
    emit_sums(flags_ref, coeffs, feature, mine_ref, theirs_ref)


def updated_basis(half_ref, own_ref, got_ref, basis):
    own, got = own_ref[...], got_ref[...]
    first = half_ref[0] == 0
    both = jnp.concatenate([jnp.where(first, own, got), jnp.where(first, got, own)], axis=0)
    r, c = basis.shape
    gram = both[:, c : c + r]
    return basis * both[:, :c] / (dot3(gram, basis, TN) + EPS)


def step_kernel(
    half_ref, own_ref, got_ref, basis_ref, feature_ref, coeffs_ref,
    newbasis_ref, newcoeffs_ref, mine_ref, theirs_ref,
):
    basis = updated_basis(half_ref, own_ref, got_ref, basis_ref[...])
    newbasis_ref[...] = basis
    feature = feature_ref[...]
    coeffs = coeffs_of(basis, coeffs_ref[...], dot(feature, basis.astype(BF), NT))
    newcoeffs_ref[...] = coeffs
    emit_sums(half_ref, coeffs, feature, mine_ref, theirs_ref)


def last_kernel(
    half_ref, own_ref, got_ref, basis_ref, feature_ref, coeffs_ref, wham_ref, walign_ref, out_ref
):
    basis = updated_basis(half_ref, own_ref, got_ref, basis_ref[...])
    feature = feature_ref[...]
    low = basis.astype(BF)
    coeffs = coeffs_of(basis, coeffs_ref[...], dot(feature, low, NT))
    rebuilt = dot(coeffs.astype(BF), low, NN).astype(BF)
    hammed = jnp.maximum(feature.astype(F32) + dot(rebuilt, wham_ref[...], NN), 0.0).astype(BF)
    out_ref[...] = dot(hammed, walign_ref[...], NN).astype(BF)


def call(kernel, outs, *args):
    scalar, whole = pl.BlockSpec(memory_space=pltpu.SMEM), pl.BlockSpec(memory_space=pltpu.VMEM)
    specs = [scalar if a.dtype == jnp.int32 else whole for a in args]
    return pl.pallas_call(
        kernel,
        out_shape=outs,
        in_specs=specs,
        out_specs=jax.tree.map(lambda _: pl.BlockSpec(memory_space=pltpu.VMEM), outs),
        compiler_params=pltpu.CompilerParams(vmem_limit_bytes=24 * 2**20),
    )(*args)


def on_device(band_input, column_taps, row_taps, w_squeeze, bases_init, w_ham, w_align):
    tile_rows, tile_cols, channels = band_input.shape
    margin = column_taps.shape[0] // 2
    index = {name: lax.axis_index(name) for name in ALL}
    half = sum(index.values()) % 2
    row, col = lax.axis_index(ROWS), lax.axis_index(COLS)
    flags = [half, col > 0, col < Z * X - 1, row > 0, row < Y * CORE - 1]
    flags = jnp.stack([f.astype(jnp.int32) for f in flags])
    sds = jax.ShapeDtypeStruct

    def ring(count, by):
        return [(i, (i + by) % count) for i in range(count)]

    width = channels // PARTS
    blocks_in_part = width // LANES

    def blocks(*dims, start=0):
        return pl.BlockSpec((*dims, LANES), lambda i: (*(0 for _ in dims), i + start))

    scalar = pl.BlockSpec(memory_space=pltpu.SMEM)
    turned, tile = blocks(tile_cols, tile_rows), blocks(tile_rows, tile_cols)
    side, edge = blocks(margin, tile_rows), blocks(margin, tile_cols)
    grid = (blocks_in_part,)
    flat = pltpu.VMEM((tile_rows * tile_cols, LANES), F32)
    params = pltpu.CompilerParams(vmem_limit_bytes=20 * 2**20)
    wide = pltpu.CompilerParams(vmem_limit_bytes=58 * 2**20)
    pixels = tile_rows * tile_cols * width
    rest = tile_rows - 2 * margin

    def cost(taps, moved):
        return pl.CostEstimate(flops=2 * taps * pixels, bytes_accessed=moved * pixels, transcendentals=0)

    whole = pl.BlockSpec(memory_space=pl.ANY)
    sides = []
    for i in range(PARTS):
        start = i * blocks_in_part
        first, last = pl.pallas_call(
            pack_kernel,
            grid=grid,
            in_specs=[blocks(tile_rows, tile_cols, start=start)],
            out_specs=[side, side],
            out_shape=[sds((margin, tile_rows, width), BF)] * 2,
            scratch_shapes=[flat],
            compiler_params=wide if i == 0 else params,
            cost_estimate=cost(1, 3),
        )(band_input)
        sides.append(
            (lax.ppermute(last, COLS, ring(Z * X, 1)), lax.ppermute(first, COLS, ring(Z * X, -1)))
        )
    own = pl.pallas_call(
        columns_own_kernel,
        grid=(channels // LANES,),
        in_specs=[tile, blocks(TAPS)],
        out_specs=turned,
        out_shape=sds((tile_cols, tile_rows, channels), F32),
        scratch_shapes=[flat, pltpu.VMEM((tile_cols, tile_rows, LANES), F32)],
        compiler_params=params,
        cost_estimate=cost(2 * TAPS, 12),
    )(band_input, column_taps)
    filtered = []
    for i in range(PARTS):
        start = i * blocks_in_part
        filtered = [
            pl.pallas_call(
                columns_rest_kernel,
                grid=grid,
                in_specs=[scalar, blocks(tile_cols, tile_rows, start=start), side, side, blocks(TAPS, start=start)] + [whole] * len(filtered),
                out_specs=blocks(tile_rows, tile_cols, start=start),
                out_shape=sds((tile_rows, tile_cols, channels), BF),
                scratch_shapes=[pltpu.VMEM((margin, tile_rows, LANES), F32)] * 2 + [flat],
                input_output_aliases={5: 0} if filtered else {},
                compiler_params=params,
                cost_estimate=cost(TAPS // 2, 6),
            )(flags, own, *sides[i], column_taps, *filtered)
        ]
    filtered = filtered[0]
    above = lax.ppermute(filtered[tile_rows - margin :], ROWS, ring(Y * CORE, 1))
    below = lax.ppermute(filtered[:margin], ROWS, ring(Y * CORE, -1))
    mid, top, low = pl.pallas_call(
        rows_own_kernel,
        grid=(channels // LANES,),
        in_specs=[tile, tile, blocks(TAPS)],
        out_specs=[blocks(rest, tile_cols), edge, edge],
        out_shape=[
            sds((rest, tile_cols, channels), BF),
            sds((margin, tile_cols, channels), F32),
            sds((margin, tile_cols, channels), F32),
        ],
        scratch_shapes=[
            pltpu.VMEM((tile_rows, tile_cols, LANES), F32),
            pltpu.VMEM((tile_rows, tile_cols, LANES), F32),
            pltpu.VMEM((rest, tile_cols, LANES), F32),
        ],
        compiler_params=params,
        cost_estimate=cost(2 * TAPS, 12),
    )(filtered, band_input, row_taps)
    n, r = tile_rows * tile_cols, bases_init.shape[1]
    packed = (r // 2, channels + LANES)
    sums = [sds(packed, F32), sds(packed, BF)]
    basis = bases_init.T
    feature, coeffs, mine, theirs = call(
        first_kernel,
        [sds((n, channels), BF), sds((n, r), F32)] + sums,
        flags, mid, top, low, above, below, row_taps, w_squeeze, basis,
    )
    for _ in range(STEPS - 1):
        own, got = summed_over_all(mine, theirs)
        basis, coeffs, mine, theirs = call(
            step_kernel,
            [sds((r, channels), F32), sds((n, r), F32)] + sums,
            flags, own, got, basis, feature, coeffs,
        )
    own, got = summed_over_all(mine, theirs)
    head_out = call(
        last_kernel,
        sds((n, channels), BF),
        flags, own, got, basis, feature, coeffs, w_ham, w_align,
    )
    return head_out.reshape(tile_rows, tile_cols, channels)


def solution(mesh):
    split = Mesh(mesh.devices.reshape(Y, CORE, Z, X), ALL)
    in_specs = (P(ROWS, COLS, None), P(), P(), P(), P(), P(), P())
    out_specs = P(ROWS, COLS, None)
    return jax.shard_map(
        on_device, mesh=split, in_specs=in_specs, out_specs=out_specs, check_vma=False
    )
```

```python
import jax
import jax.numpy as jnp
from jax import lax
from jax.experimental import pallas as pl
from jax.experimental.pallas import tpu as pltpu
from jax.sharding import Mesh
from jax.sharding import PartitionSpec as P

STEPS = 3
Y, CORE, Z, X = 4, 2, 8, 4
ROWS = ("y", "core")
COLS = ("z", "x")
ALL = ("y", "core", "z", "x")
EPS = 1e-06
BF = jnp.bfloat16
F32 = jnp.float32


TAPS = 21
MARGIN = TAPS // 2
LANES = 128


def weighted(taps_ref, items, rows):
    outs = [None] * len(items)
    for k in range(TAPS):
        if not any(k in pairs for pairs in items):
            continue
        tap = jnp.broadcast_to(taps_ref[k : k + 1, :], (rows, LANES))
        for i, pairs in enumerate(items):
            if k in pairs:
                term = tap * pairs[k]
                outs[i] = term if outs[i] is None else outs[i] + term
    return outs


def own_sums(taps_ref, load, length, group, emit):
    for start in range(0, length, group):
        lo, hi = max(0, start - MARGIN), min(length, start + group + MARGIN)
        window = {i: load(i) for i in range(lo, hi)}
        items = [
            {k: window[o + k - MARGIN] for k in range(TAPS) if o + k - MARGIN in window}
            for o in range(start, start + group)
        ]
        for i, value in enumerate(weighted(taps_ref, items, 8)):
            emit(start + i, value)


def columns_own_kernel(band_ref, taps_ref, out_ref, flat, turned):
    h, w, lanes = band_ref.shape
    flat[...] = band_ref[...].astype(F32).reshape(h * w, lanes)
    for j in range(w):
        turned[j] = flat[pl.ds(j, h, stride=w), :]

    def body(i, carry):
        rows = pl.ds(pl.multiple_of(i * 8, 8), 8)

        def emit(o, value):
            out_ref[o, rows, :] = value

        own_sums(taps_ref, lambda j: turned[j, rows, :], w, 8, emit)
        return carry

    lax.fori_loop(0, h // 8, body, 0)


def columns_rest_kernel(flags_ref, own_ref, left_ref, right_ref, taps_ref, out_ref, lefts, rights, flat):
    w, h, lanes = own_ref.shape
    lefts[...] = jnp.where(flags_ref[1] == 1, left_ref[...].astype(F32), 0.0)
    rights[...] = jnp.where(flags_ref[2] == 1, right_ref[...].astype(F32), 0.0)

    def body(i, carry):
        rows = pl.ds(pl.multiple_of(i * 8, 8), 8)

        def put(o, value):
            flat[pl.ds(i * (8 * w) + o, 8, stride=w), :] = value

        before = [lefts[j, rows, :] for j in range(MARGIN)]
        items = [{j - o: before[j] for j in range(o, MARGIN)} for o in range(MARGIN)]
        for o, value in enumerate(weighted(taps_ref, items, 8)):
            put(o, own_ref[o, rows, :] + value)
        for o in range(MARGIN, w - MARGIN):
            put(o, own_ref[o, rows, :])
        after = [rights[j, rows, :] for j in range(MARGIN)]
        items = [{2 * MARGIN + j - o: after[j] for j in range(o + 1)} for o in range(MARGIN)]
        for o, value in enumerate(weighted(taps_ref, items, 8)):
            put(w - MARGIN + o, own_ref[w - MARGIN + o, rows, :] + value)
        return carry

    lax.fori_loop(0, h // 8, body, 0)
    out_ref[...] = flat[...].reshape(h, w, lanes).astype(BF)


def rows_own_kernel(filtered_ref, band_ref, taps_ref, mid_ref, top_ref, low_ref, source, residual, mixed):
    h, w, _ = filtered_ref.shape
    source[...] = filtered_ref[...].astype(F32)
    residual[...] = band_ref[...].astype(F32)

    def body(i, carry):
        cols = pl.ds(pl.multiple_of(i * 8, 8), 8)

        def emit(o, value):
            value = residual[o, cols, :] + value
            if o < MARGIN:
                top_ref[o, cols, :] = value
            elif o >= h - MARGIN:
                low_ref[o - (h - MARGIN), cols, :] = value
            else:
                mixed[o - MARGIN, cols, :] = value

        own_sums(taps_ref, lambda j: source[j, cols, :], h, 8, emit)
        return carry

    lax.fori_loop(0, w // 8, body, 0)
    mid_ref[...] = mixed[...].astype(BF)


def finished_edge(part_ref, halo_ref, taps_ref, present, pairs_of):
    blocks = []
    for start in range(0, part_ref.shape[2], LANES):
        lanes = slice(start, start + LANES)
        halo = [
            jnp.where(present, halo_ref[j, :, lanes].astype(F32), 0.0) for j in range(MARGIN)
        ]
        rows = []
        for o in range(MARGIN):
            value = part_ref[o, :, lanes]
            for k, j in pairs_of(o):
                value = value + taps_ref[k : k + 1, lanes] * halo[j]
            rows.append(value.astype(BF))
        blocks.append(jnp.concatenate(rows, axis=0))
    return jnp.concatenate(blocks, axis=1)


def pair_4a(i):
    return i ^ 1


def pair_4b(i):
    return 3 - i


def pair_8a(i):
    return i ^ 1


def pair_8b(i):
    return (i + 1) % 8 if i % 2 else (i - 1) % 8


def pair_8c(i):
    return (3, 6, 5, 0, 7, 2, 1, 4)[i]


ROUNDS = [
    ("x", pair_4a), ("x", pair_4b), ("y", pair_4a), ("y", pair_4b),
    ("z", pair_8a), ("z", pair_8b), ("z", pair_8c),
]


def round_pairs(axis, rule):
    pairs = []
    for y in range(Y):
        for core in range(CORE):
            for z in range(Z):
                for x in range(X):
                    at = {"y": y, "core": core, "z": z, "x": x}
                    to = dict(at, core=1 - core)
                    to[axis] = rule(at[axis])
                    pairs.append(
                        tuple(((p["y"] * CORE + p["core"]) * Z + p["z"]) * X + p["x"] for p in (at, to))
                    )
    return pairs


def summed_over_all(mine, theirs):
    swap = [(0, 1), (1, 0)]
    total = mine + lax.ppermute(theirs, "core", swap).astype(F32)
    for axis, rule in ROUNDS:
        total = lax.optimization_barrier(total)
        got = lax.ppermute(total.astype(BF), ALL, round_pairs(axis, rule))
        total = total + got.astype(F32)
    return total, lax.ppermute(total, "core", swap)


def split3(a):
    hi = a.astype(BF)
    return hi, (a - hi.astype(F32)).astype(BF)


def dot(a, b, dims):
    return lax.dot_general(a, b, (dims, ((), ())), preferred_element_type=F32)


def dot3(a, b, dims):
    ah, al = split3(a)
    bh, bl = split3(b)
    return dot(ah, bh, dims) + (dot(ah, bl, dims) + dot(al, bh, dims))


NN = ((1,), (0,))
NT = ((1,), (1,))
TN = ((0,), (0,))


def coeffs_of(basis, coeffs, numerator):
    gram = dot3(basis, basis, NT)
    return coeffs * numerator / (dot3(gram, coeffs, NN) + EPS)


def emit_sums(half_ref, coeffs, feature, mine_ref, theirs_ref):
    c, rows = feature.shape[1], mine_ref.shape[0]
    first = half_ref[0] == 0
    num = dot(coeffs.astype(BF), feature, NN)
    mine_ref[:, :c] = jnp.where(first, num[:rows], num[rows:])
    theirs_ref[:, :c] = jnp.where(first, num[rows:], num[:rows]).astype(BF)
    gram = dot3(coeffs, coeffs, NT)
    gram = jnp.concatenate([gram, jnp.zeros_like(gram)], axis=1)
    mine_ref[:, c:] = jnp.where(first, gram[:rows], gram[rows:])
    theirs_ref[:, c:] = jnp.where(first, gram[rows:], gram[:rows]).astype(BF)


def first_kernel(
    flags_ref, mid_ref, top_ref, low_ref, near_ref, far_ref, taps_ref, w_ref, basis_ref,
    feature_ref, coeffs_ref, mine_ref, theirs_ref,
):
    rows, cols, channels = mid_ref.shape
    edge, mid = MARGIN * cols, rows * cols
    w = w_ref[...]

    def squeezed(mixed):
        return jnp.maximum(dot(mixed, w, NN), 0.0).astype(BF)

    for core, (above_ref, below_ref) in enumerate(((far_ref, near_ref), (near_ref, far_ref))):

        @pl.when(flags_ref[5] == core)
        def _(above_ref=above_ref, below_ref=below_ref):
            top = finished_edge(
                top_ref, above_ref, taps_ref, flags_ref[3] == 1,
                lambda o: [(j - o, j) for j in range(o, MARGIN)],
            )
            low = finished_edge(
                low_ref, below_ref, taps_ref, flags_ref[4] == 1,
                lambda o: [(2 * MARGIN + j - o, j) for j in range(o + 1)],
            )
            feature_ref[:edge] = squeezed(top)
            feature_ref[edge + mid :] = squeezed(low)

    feature_ref[edge : edge + mid] = squeezed(mid_ref[...].reshape(mid, channels))
    feature = feature_ref[...]
    basis = basis_ref[...]
    scores = dot(basis.astype(BF), feature, NT)
    e = jnp.exp(scores - jnp.max(scores, axis=0, keepdims=True))
    soft = e / jnp.sum(e, axis=0, keepdims=True)
    coeffs = coeffs_of(basis, soft, scores)
    coeffs_ref[...] = coeffs
    emit_sums(flags_ref, coeffs, feature, mine_ref, theirs_ref)


def updated_basis(half_ref, own_ref, got_ref, basis):
    own, got = own_ref[...], got_ref[...]
    first = half_ref[0] == 0
    both = jnp.concatenate([jnp.where(first, own, got), jnp.where(first, got, own)], axis=0)
    r, c = basis.shape
    gram = both[:, c : c + r]
    return basis * both[:, :c] / (dot3(gram, basis, TN) + EPS)


def step_kernel(
    half_ref, own_ref, got_ref, basis_ref, feature_ref, coeffs_ref,
    newbasis_ref, newcoeffs_ref, mine_ref, theirs_ref,
):
    basis = updated_basis(half_ref, own_ref, got_ref, basis_ref[...])
    newbasis_ref[...] = basis
    feature = feature_ref[...]
    coeffs = coeffs_of(basis, coeffs_ref[...], dot(basis.astype(BF), feature, NT))
    newcoeffs_ref[...] = coeffs
    emit_sums(half_ref, coeffs, feature, mine_ref, theirs_ref)


def last_kernel(
    half_ref, own_ref, got_ref, basis_ref, feature_ref, coeffs_ref, wham_ref, walign_ref, out_ref
):
    basis = updated_basis(half_ref, own_ref, got_ref, basis_ref[...])
    feature = feature_ref[...]
    low = basis.astype(BF)
    coeffs = coeffs_of(basis, coeffs_ref[...], dot(low, feature, NT))
    rebuilt = dot(coeffs.astype(BF), low, TN).astype(BF)
    hammed = jnp.maximum(feature.astype(F32) + dot(rebuilt, wham_ref[...], NN), 0.0).astype(BF)
    out_ref[...] = dot(hammed, walign_ref[...], NN).astype(BF)


def call(kernel, outs, *args):
    scalar, whole = pl.BlockSpec(memory_space=pltpu.SMEM), pl.BlockSpec(memory_space=pltpu.VMEM)
    specs = [scalar if a.dtype == jnp.int32 else whole for a in args]
    return pl.pallas_call(
        kernel,
        out_shape=outs,
        in_specs=specs,
        out_specs=jax.tree.map(lambda _: pl.BlockSpec(memory_space=pltpu.VMEM), outs),
        compiler_params=pltpu.CompilerParams(vmem_limit_bytes=24 * 2**20),
    )(*args)


def on_device(band_input, column_taps, row_taps, w_squeeze, bases_init, w_ham, w_align):
    tile_rows, tile_cols, channels = band_input.shape
    margin = column_taps.shape[0] // 2
    index = {name: lax.axis_index(name) for name in ALL}
    half = sum(index.values()) % 2
    row, col = lax.axis_index(ROWS), lax.axis_index(COLS)
    flags = [half, col > 0, col < Z * X - 1, row > 0, row < Y * CORE - 1, index["core"]]
    flags = jnp.stack([f.astype(jnp.int32) for f in flags])
    sds = jax.ShapeDtypeStruct

    def ring(count, by):
        return [(i, (i + by) % count) for i in range(count)]

    left = band_input[:, tile_cols - margin :].transpose(1, 0, 2)
    right = band_input[:, :margin].transpose(1, 0, 2)
    left = lax.ppermute(left, COLS, ring(Z * X, 1))
    right = lax.ppermute(right, COLS, ring(Z * X, -1))

    def blocks(*dims):
        return pl.BlockSpec((*dims, LANES), lambda i: (*(0 for _ in dims), i))

    scalar = pl.BlockSpec(memory_space=pltpu.SMEM)
    tile, turned = blocks(tile_rows, tile_cols), blocks(tile_cols, tile_rows)
    side, edge = blocks(margin, tile_rows), blocks(margin, tile_cols)
    taps = blocks(TAPS)
    grid = (channels // LANES,)
    flat = pltpu.VMEM((tile_rows * tile_cols, LANES), F32)
    params = pltpu.CompilerParams(vmem_limit_bytes=20 * 2**20)
    pixels = tile_rows * tile_cols * channels
    cost = pl.CostEstimate(flops=2 * TAPS * pixels, bytes_accessed=6 * pixels, transcendentals=0)
    own = pl.pallas_call(
        columns_own_kernel,
        grid=grid,
        in_specs=[tile, taps],
        out_specs=turned,
        out_shape=sds((tile_cols, tile_rows, channels), F32),
        scratch_shapes=[flat, pltpu.VMEM((tile_cols, tile_rows, LANES), F32)],
        compiler_params=params,
        cost_estimate=cost,
    )(band_input, column_taps)
    filtered = pl.pallas_call(
        columns_rest_kernel,
        grid=grid,
        in_specs=[scalar, turned, side, side, taps],
        out_specs=tile,
        out_shape=sds(band_input.shape, BF),
        scratch_shapes=[pltpu.VMEM((margin, tile_rows, LANES), F32)] * 2 + [flat],
        compiler_params=params,
    )(flags, own, left, right, column_taps)
    bottom = tile_rows - margin
    even = index["core"] == 0
    to_far = lax.dynamic_slice_in_dim(filtered, jnp.where(even, 0, bottom), margin)
    to_near = lax.dynamic_slice_in_dim(filtered, jnp.where(even, bottom, 0), margin)
    chips = [(i, (i + 1) % (Y * CORE)) for i in range(1, Y * CORE, 2)]
    far = lax.ppermute(to_far, ROWS, chips + [(j, i) for i, j in chips])
    near = lax.ppermute(to_near, "core", [(0, 1), (1, 0)])
    rest = tile_rows - 2 * margin
    mid, top, low = pl.pallas_call(
        rows_own_kernel,
        grid=grid,
        in_specs=[tile, tile, taps],
        out_specs=[blocks(rest, tile_cols), edge, edge],
        out_shape=[
            sds((rest, tile_cols, channels), BF),
            sds((margin, tile_cols, channels), F32),
            sds((margin, tile_cols, channels), F32),
        ],
        scratch_shapes=[
            pltpu.VMEM((tile_rows, tile_cols, LANES), F32),
            pltpu.VMEM((tile_rows, tile_cols, LANES), F32),
            pltpu.VMEM((rest, tile_cols, LANES), F32),
        ],
        compiler_params=params,
        cost_estimate=cost,
    )(filtered, band_input, row_taps)
    n, r = tile_rows * tile_cols, bases_init.shape[1]
    width = channels + 128
    sums = [sds((r // 2, width), F32), sds((r // 2, width), BF)]
    basis = bases_init.T
    feature, coeffs, mine, theirs = call(
        first_kernel,
        [sds((n, channels), BF), sds((r, n), F32)] + sums,
        flags, mid, top, low, near, far, row_taps, w_squeeze, basis,
    )
    for _ in range(STEPS - 1):
        own, got = summed_over_all(mine, theirs)
        basis, coeffs, mine, theirs = call(
            step_kernel,
            [sds((r, channels), F32), sds((r, n), F32)] + sums,
            flags, own, got, basis, feature, coeffs,
        )
    own, got = summed_over_all(mine, theirs)
    head_out = call(
        last_kernel,
        sds((n, channels), BF),
        flags, own, got, basis, feature, coeffs, w_ham, w_align,
    )
    return head_out.reshape(tile_rows, tile_cols, channels)


def solution(mesh):
    split = Mesh(mesh.devices.reshape(Y, CORE, Z, X), ALL)
    in_specs = (P(ROWS, COLS, None), P(), P(), P(), P(), P(), P())
    out_specs = P(ROWS, COLS, None)
    return jax.shard_map(
        on_device, mesh=split, in_specs=in_specs, out_specs=out_specs, check_vma=False
    )
```

```python
import jax
import jax.numpy as jnp
from jax import lax
from jax.experimental import pallas as pl
from jax.experimental.pallas import tpu as pltpu
from jax.sharding import Mesh
from jax.sharding import PartitionSpec as P

STEPS = 3
Y, CORE, Z, X = 4, 2, 8, 4
ROWS = ("y", "core")
COLS = ("z", "x")
ALL = ("y", "core", "z", "x")
EPS = 1e-06
BF = jnp.bfloat16
F32 = jnp.float32


TAPS = 21
MARGIN = TAPS // 2
LANES = 128


def weighted(taps_ref, items, rows):
    outs = [None] * len(items)
    for k in range(TAPS):
        if not any(k in pairs for pairs in items):
            continue
        tap = jnp.broadcast_to(taps_ref[k : k + 1, :], (rows, LANES))
        for i, pairs in enumerate(items):
            if k in pairs:
                term = tap * pairs[k]
                outs[i] = term if outs[i] is None else outs[i] + term
    return outs


def own_sums(taps_ref, load, length, group, emit):
    for start in range(0, length, group):
        lo, hi = max(0, start - MARGIN), min(length, start + group + MARGIN)
        window = {i: load(i) for i in range(lo, hi)}
        items = [
            {k: window[o + k - MARGIN] for k in range(TAPS) if o + k - MARGIN in window}
            for o in range(start, start + group)
        ]
        for i, value in enumerate(weighted(taps_ref, items, 8)):
            emit(start + i, value)


def columns_own_kernel(band_ref, taps_ref, out_ref, flat, turned):
    h, w, lanes = band_ref.shape
    flat[...] = band_ref[...].astype(F32).reshape(h * w, lanes)
    for j in range(w):
        turned[j] = flat[pl.ds(j, h, stride=w), :]

    def body(i, carry):
        rows = pl.ds(pl.multiple_of(i * 8, 8), 8)

        def emit(o, value):
            flat[pl.ds(i * (8 * w) + o, 8, stride=w), :] = value

        own_sums(taps_ref, lambda j: turned[j, rows, :], w, 8, emit)
        return carry

    lax.fori_loop(0, h // 8, body, 0)
    out_ref[...] = flat[...].reshape(h, w, lanes)


def columns_rest_kernel(flags_ref, own_ref, left_ref, right_ref, taps_ref, out_ref, lefts, rights, flat):
    h, w, lanes = own_ref.shape
    lefts[...] = jnp.where(flags_ref[1] == 1, left_ref[...].astype(F32), 0.0)
    rights[...] = jnp.where(flags_ref[2] == 1, right_ref[...].astype(F32), 0.0)

    @pl.when(pl.program_id(0) == 0)
    def _():
        flat[...] = jnp.zeros_like(flat)

    def body(i, carry):
        rows = pl.ds(pl.multiple_of(i * 8, 8), 8)

        def put(o, value):
            flat[pl.ds(i * (8 * w) + o, 8, stride=w), :] = value

        before = [lefts[j, rows, :] for j in range(MARGIN)]
        items = [{j - o: before[j] for j in range(o, MARGIN)} for o in range(MARGIN)]
        for o, value in enumerate(weighted(taps_ref, items, 8)):
            put(o, value)
        after = [rights[j, rows, :] for j in range(MARGIN)]
        items = [{2 * MARGIN + j - o: after[j] for j in range(o + 1)} for o in range(MARGIN)]
        for o, value in enumerate(weighted(taps_ref, items, 8)):
            put(w - MARGIN + o, value)
        return carry

    lax.fori_loop(0, h // 8, body, 0)
    out_ref[...] = (own_ref[...] + flat[...].reshape(h, w, lanes)).astype(BF)


def rows_own_kernel(filtered_ref, band_ref, taps_ref, mid_ref, top_ref, low_ref, source, residual, mixed):
    h, w, _ = filtered_ref.shape
    source[...] = filtered_ref[...].astype(F32)
    residual[...] = band_ref[...].astype(F32)

    def body(i, carry):
        cols = pl.ds(pl.multiple_of(i * 8, 8), 8)

        def emit(o, value):
            value = residual[o, cols, :] + value
            if o < MARGIN:
                top_ref[o, cols, :] = value
            elif o >= h - MARGIN:
                low_ref[o - (h - MARGIN), cols, :] = value
            else:
                mixed[o - MARGIN, cols, :] = value

        own_sums(taps_ref, lambda j: source[j, cols, :], h, 8, emit)
        return carry

    lax.fori_loop(0, w // 8, body, 0)
    mid_ref[...] = mixed[...].astype(BF)


def finished_edge(part_ref, halo_ref, taps_ref, present, pairs_of):
    blocks = []
    for start in range(0, part_ref.shape[2], LANES):
        lanes = slice(start, start + LANES)
        halo = [
            jnp.where(present, halo_ref[j, :, lanes].astype(F32), 0.0) for j in range(MARGIN)
        ]
        rows = []
        for o in range(MARGIN):
            value = part_ref[o, :, lanes]
            for k, j in pairs_of(o):
                value = value + taps_ref[k : k + 1, lanes] * halo[j]
            rows.append(value.astype(BF))
        blocks.append(jnp.concatenate(rows, axis=0))
    return jnp.concatenate(blocks, axis=1)


def pair_4a(i):
    return i ^ 1


def pair_4b(i):
    return 3 - i


def pair_8a(i):
    return i ^ 1


def pair_8b(i):
    return (i + 1) % 8 if i % 2 else (i - 1) % 8


def pair_8c(i):
    return (3, 6, 5, 0, 7, 2, 1, 4)[i]


ROUNDS = [
    ("x", pair_4a), ("x", pair_4b), ("y", pair_4a), ("y", pair_4b),
    ("z", pair_8a), ("z", pair_8b), ("z", pair_8c),
]


def round_pairs(axis, rule):
    pairs = []
    for y in range(Y):
        for core in range(CORE):
            for z in range(Z):
                for x in range(X):
                    at = {"y": y, "core": core, "z": z, "x": x}
                    to = dict(at, core=1 - core)
                    to[axis] = rule(at[axis])
                    pairs.append(
                        tuple(((p["y"] * CORE + p["core"]) * Z + p["z"]) * X + p["x"] for p in (at, to))
                    )
    return pairs


def summed_over_all(mine, theirs):
    swap = [(0, 1), (1, 0)]
    total = mine + lax.ppermute(theirs, "core", swap).astype(F32)
    for axis, rule in ROUNDS:
        total = lax.optimization_barrier(total)
        got = lax.ppermute(total.astype(BF), ALL, round_pairs(axis, rule))
        total = total + got.astype(F32)
    return total, lax.ppermute(total, "core", swap)


def split3(a):
    hi = a.astype(BF)
    return hi, (a - hi.astype(F32)).astype(BF)


def dot(a, b, dims):
    return lax.dot_general(a, b, (dims, ((), ())), preferred_element_type=F32)


def dot3(a, b, dims):
    ah, al = split3(a)
    bh, bl = split3(b)
    return dot(ah, bh, dims) + (dot(ah, bl, dims) + dot(al, bh, dims))


NN = ((1,), (0,))
NT = ((1,), (1,))
TN = ((0,), (0,))


def coeffs_of(basis, coeffs, numerator):
    gram = dot3(basis, basis, NT)
    return coeffs * numerator / (dot3(gram, coeffs, NN) + EPS)


def emit_sums(half_ref, coeffs, feature, mine_ref, theirs_ref):
    c, rows = feature.shape[1], mine_ref.shape[0]
    first = half_ref[0] == 0
    num = dot(coeffs.astype(BF), feature, NN)
    mine_ref[:, :c] = jnp.where(first, num[:rows], num[rows:])
    theirs_ref[:, :c] = jnp.where(first, num[rows:], num[:rows]).astype(BF)
    gram = dot3(coeffs, coeffs, NT)
    gram = jnp.concatenate([gram, jnp.zeros_like(gram)], axis=1)
    mine_ref[:, c:] = jnp.where(first, gram[:rows], gram[rows:])
    theirs_ref[:, c:] = jnp.where(first, gram[rows:], gram[:rows]).astype(BF)


def first_kernel(
    flags_ref, mid_ref, top_ref, low_ref, above_ref, below_ref, taps_ref, w_ref, basis_ref,
    feature_ref, coeffs_ref, mine_ref, theirs_ref,
):
    rows, cols, channels = mid_ref.shape
    edge, mid = MARGIN * cols, rows * cols
    w = w_ref[...]
    top = finished_edge(
        top_ref, above_ref, taps_ref, flags_ref[3] == 1, lambda o: [(j - o, j) for j in range(o, MARGIN)]
    )
    low = finished_edge(
        low_ref, below_ref, taps_ref, flags_ref[4] == 1, lambda o: [(2 * MARGIN + j - o, j) for j in range(o + 1)]
    )

    def squeezed(mixed):
        return jnp.maximum(dot(mixed, w, NN), 0.0).astype(BF)

    feature_ref[:edge] = squeezed(top)
    feature_ref[edge : edge + mid] = squeezed(mid_ref[...].reshape(mid, channels))
    feature_ref[edge + mid :] = squeezed(low)
    feature = feature_ref[...]
    basis = basis_ref[...]
    scores = dot(basis.astype(BF), feature, NT)
    e = jnp.exp(scores - jnp.max(scores, axis=0, keepdims=True))
    soft = e / jnp.sum(e, axis=0, keepdims=True)
    coeffs = coeffs_of(basis, soft, scores)
    coeffs_ref[...] = coeffs
    emit_sums(flags_ref, coeffs, feature, mine_ref, theirs_ref)


def updated_basis(half_ref, own_ref, got_ref, basis):
    own, got = own_ref[...], got_ref[...]
    first = half_ref[0] == 0
    both = jnp.concatenate([jnp.where(first, own, got), jnp.where(first, got, own)], axis=0)
    r, c = basis.shape
    gram = both[:, c : c + r]
    return basis * both[:, :c] / (dot3(gram, basis, TN) + EPS)


def step_kernel(
    half_ref, own_ref, got_ref, basis_ref, feature_ref, coeffs_ref,
    newbasis_ref, newcoeffs_ref, mine_ref, theirs_ref,
):
    basis = updated_basis(half_ref, own_ref, got_ref, basis_ref[...])
    newbasis_ref[...] = basis
    feature = feature_ref[...]
    coeffs = coeffs_of(basis, coeffs_ref[...], dot(basis.astype(BF), feature, NT))
    newcoeffs_ref[...] = coeffs
    emit_sums(half_ref, coeffs, feature, mine_ref, theirs_ref)


def last_kernel(
    half_ref, own_ref, got_ref, basis_ref, feature_ref, coeffs_ref, wham_ref, walign_ref, out_ref
):
    basis = updated_basis(half_ref, own_ref, got_ref, basis_ref[...])
    feature = feature_ref[...]
    low = basis.astype(BF)
    coeffs = coeffs_of(basis, coeffs_ref[...], dot(low, feature, NT))
    rebuilt = dot(coeffs.astype(BF), low, TN).astype(BF)
    hammed = jnp.maximum(feature.astype(F32) + dot(rebuilt, wham_ref[...], NN), 0.0).astype(BF)
    out_ref[...] = dot(hammed, walign_ref[...], NN).astype(BF)


def call(kernel, outs, *args):
    scalar, whole = pl.BlockSpec(memory_space=pltpu.SMEM), pl.BlockSpec(memory_space=pltpu.VMEM)
    specs = [scalar if a.dtype == jnp.int32 else whole for a in args]
    return pl.pallas_call(
        kernel,
        out_shape=outs,
        in_specs=specs,
        out_specs=jax.tree.map(lambda _: pl.BlockSpec(memory_space=pltpu.VMEM), outs),
        compiler_params=pltpu.CompilerParams(vmem_limit_bytes=24 * 2**20),
    )(*args)


def on_device(band_input, column_taps, row_taps, w_squeeze, bases_init, w_ham, w_align):
    tile_rows, tile_cols, channels = band_input.shape
    margin = column_taps.shape[0] // 2
    index = {name: lax.axis_index(name) for name in ALL}
    half = sum(index.values()) % 2
    row, col = lax.axis_index(ROWS), lax.axis_index(COLS)
    flags = [half, col > 0, col < Z * X - 1, row > 0, row < Y * CORE - 1]
    flags = jnp.stack([f.astype(jnp.int32) for f in flags])
    sds = jax.ShapeDtypeStruct

    def ring(count, by):
        return [(i, (i + by) % count) for i in range(count)]

    left = band_input[:, tile_cols - margin :].transpose(1, 0, 2)
    right = band_input[:, :margin].transpose(1, 0, 2)
    left = lax.ppermute(left, COLS, ring(Z * X, 1))
    right = lax.ppermute(right, COLS, ring(Z * X, -1))

    def blocks(*dims):
        return pl.BlockSpec((*dims, LANES), lambda i: (*(0 for _ in dims), i))

    scalar = pl.BlockSpec(memory_space=pltpu.SMEM)
    tile = blocks(tile_rows, tile_cols)
    side, edge = blocks(margin, tile_rows), blocks(margin, tile_cols)
    taps = blocks(TAPS)
    grid = (channels // LANES,)
    flat = pltpu.VMEM((tile_rows * tile_cols, LANES), F32)
    params = pltpu.CompilerParams(vmem_limit_bytes=20 * 2**20)
    pixels = tile_rows * tile_cols * channels
    cost = pl.CostEstimate(flops=2 * TAPS * pixels, bytes_accessed=6 * pixels, transcendentals=0)
    own = pl.pallas_call(
        columns_own_kernel,
        grid=grid,
        in_specs=[tile, taps],
        out_specs=tile,
        out_shape=sds(band_input.shape, F32),
        scratch_shapes=[flat, pltpu.VMEM((tile_cols, tile_rows, LANES), F32)],
        compiler_params=params,
        cost_estimate=cost,
    )(band_input, column_taps)
    filtered = pl.pallas_call(
        columns_rest_kernel,
        grid=grid,
        in_specs=[scalar, tile, side, side, taps],
        out_specs=tile,
        out_shape=sds(band_input.shape, BF),
        scratch_shapes=[pltpu.VMEM((margin, tile_rows, LANES), F32)] * 2 + [flat],
        compiler_params=params,
    )(flags, own, left, right, column_taps)
    above = lax.ppermute(filtered[tile_rows - margin :], ROWS, ring(Y * CORE, 1))
    below = lax.ppermute(filtered[:margin], ROWS, ring(Y * CORE, -1))
    rest = tile_rows - 2 * margin
    mid, top, low = pl.pallas_call(
        rows_own_kernel,
        grid=grid,
        in_specs=[tile, tile, taps],
        out_specs=[blocks(rest, tile_cols), edge, edge],
        out_shape=[
            sds((rest, tile_cols, channels), BF),
            sds((margin, tile_cols, channels), F32),
            sds((margin, tile_cols, channels), F32),
        ],
        scratch_shapes=[
            pltpu.VMEM((tile_rows, tile_cols, LANES), F32),
            pltpu.VMEM((tile_rows, tile_cols, LANES), F32),
            pltpu.VMEM((rest, tile_cols, LANES), F32),
        ],
        compiler_params=params,
        cost_estimate=cost,
    )(filtered, band_input, row_taps)
    n, r = tile_rows * tile_cols, bases_init.shape[1]
    width = channels + 128
    sums = [sds((r // 2, width), F32), sds((r // 2, width), BF)]
    basis = bases_init.T
    feature, coeffs, mine, theirs = call(
        first_kernel,
        [sds((n, channels), BF), sds((r, n), F32)] + sums,
        flags, mid, top, low, above, below, row_taps, w_squeeze, basis,
    )
    for _ in range(STEPS - 1):
        own, got = summed_over_all(mine, theirs)
        basis, coeffs, mine, theirs = call(
            step_kernel,
            [sds((r, channels), F32), sds((r, n), F32)] + sums,
            flags, own, got, basis, feature, coeffs,
        )
    own, got = summed_over_all(mine, theirs)
    head_out = call(
        last_kernel,
        sds((n, channels), BF),
        flags, own, got, basis, feature, coeffs, w_ham, w_align,
    )
    return head_out.reshape(tile_rows, tile_cols, channels)


def solution(mesh):
    split = Mesh(mesh.devices.reshape(Y, CORE, Z, X), ALL)
    in_specs = (P(ROWS, COLS, None), P(), P(), P(), P(), P(), P())
    out_specs = P(ROWS, COLS, None)
    return jax.shard_map(
        on_device, mesh=split, in_specs=in_specs, out_specs=out_specs, check_vma=False
    )
```

```python
import jax
import jax.numpy as jnp
from jax import lax
from jax.experimental import pallas as pl
from jax.experimental.pallas import tpu as pltpu
from jax.sharding import Mesh
from jax.sharding import PartitionSpec as P

STEPS = 3
Y, CORE, Z, X = 4, 2, 8, 4
ROWS = ("y", "core")
COLS = ("z", "x")
ALL = ("y", "core", "z", "x")
EPS = 1e-06
BF = jnp.bfloat16
F32 = jnp.float32


TAPS = 21
MARGIN = TAPS // 2
LANES = 128


def weighted(taps_ref, items, rows):
    outs = [None] * len(items)
    for k in range(TAPS):
        if not any(k in pairs for pairs in items):
            continue
        tap = jnp.broadcast_to(taps_ref[k : k + 1, :], (rows, LANES))
        for i, pairs in enumerate(items):
            if k in pairs:
                term = tap * pairs[k]
                outs[i] = term if outs[i] is None else outs[i] + term
    return outs


def own_sums(taps_ref, load, length, group, emit):
    for start in range(0, length, group):
        lo, hi = max(0, start - MARGIN), min(length, start + group + MARGIN)
        window = {i: load(i) for i in range(lo, hi)}
        items = [
            {k: window[o + k - MARGIN] for k in range(TAPS) if o + k - MARGIN in window}
            for o in range(start, start + group)
        ]
        for i, value in enumerate(weighted(taps_ref, items, 8)):
            emit(start + i, value)


def pack_kernel(band_ref, first_ref, last_ref, flat):
    h, w, channels = band_ref.shape
    for t in range(channels // LANES):
        lanes = slice(t * LANES, (t + 1) * LANES)
        flat[t] = band_ref[:, :, lanes].astype(F32).reshape(h * w, LANES)
        for j in range(MARGIN):
            first_ref[j, :, lanes] = flat[t, pl.ds(j, h, stride=w), :].astype(BF)
            last_ref[j, :, lanes] = flat[t, pl.ds(w - MARGIN + j, h, stride=w), :].astype(BF)


def columns_own_kernel(band_ref, taps_ref, out_ref, flat, turned):
    h, w, lanes = band_ref.shape
    flat[...] = band_ref[...].astype(F32).reshape(h * w, lanes)
    for j in range(w):
        turned[j] = flat[pl.ds(j, h, stride=w), :]

    def body(i, carry):
        rows = pl.ds(pl.multiple_of(i * 8, 8), 8)

        def emit(o, value):
            flat[pl.ds(i * (8 * w) + o, 8, stride=w), :] = value

        own_sums(taps_ref, lambda j: turned[j, rows, :], w, 8, emit)
        return carry

    lax.fori_loop(0, h // 8, body, 0)
    out_ref[...] = flat[...].reshape(h, w, lanes)


def columns_rest_kernel(flags_ref, own_ref, left_ref, right_ref, taps_ref, out_ref, lefts, rights, flat):
    h, w, lanes = own_ref.shape
    lefts[...] = jnp.where(flags_ref[1] == 1, left_ref[...].astype(F32), 0.0)
    rights[...] = jnp.where(flags_ref[2] == 1, right_ref[...].astype(F32), 0.0)

    @pl.when(pl.program_id(0) == 0)
    def _():
        flat[...] = jnp.zeros_like(flat)

    def body(i, carry):
        rows = pl.ds(pl.multiple_of(i * 8, 8), 8)

        def put(o, value):
            flat[pl.ds(i * (8 * w) + o, 8, stride=w), :] = value

        before = [lefts[j, rows, :] for j in range(MARGIN)]
        items = [{j - o: before[j] for j in range(o, MARGIN)} for o in range(MARGIN)]
        for o, value in enumerate(weighted(taps_ref, items, 8)):
            put(o, value)
        after = [rights[j, rows, :] for j in range(MARGIN)]
        items = [{2 * MARGIN + j - o: after[j] for j in range(o + 1)} for o in range(MARGIN)]
        for o, value in enumerate(weighted(taps_ref, items, 8)):
            put(w - MARGIN + o, value)
        return carry

    lax.fori_loop(0, h // 8, body, 0)
    out_ref[...] = (own_ref[...] + flat[...].reshape(h, w, lanes)).astype(BF)


def rows_own_kernel(filtered_ref, band_ref, taps_ref, mid_ref, top_ref, low_ref, source, residual, mixed):
    h, w, _ = filtered_ref.shape
    source[...] = filtered_ref[...].astype(F32)
    residual[...] = band_ref[...].astype(F32)

    def body(i, carry):
        cols = pl.ds(pl.multiple_of(i * 8, 8), 8)

        def emit(o, value):
            value = residual[o, cols, :] + value
            if o < MARGIN:
                top_ref[o, cols, :] = value
            elif o >= h - MARGIN:
                low_ref[o - (h - MARGIN), cols, :] = value
            else:
                mixed[o - MARGIN, cols, :] = value

        own_sums(taps_ref, lambda j: source[j, cols, :], h, 8, emit)
        return carry

    lax.fori_loop(0, w // 8, body, 0)
    mid_ref[...] = mixed[...].astype(BF)


def finished_edge(part_ref, halo_ref, taps_ref, present, pairs_of):
    blocks = []
    for start in range(0, part_ref.shape[2], LANES):
        lanes = slice(start, start + LANES)
        halo = [
            jnp.where(present, halo_ref[j, :, lanes].astype(F32), 0.0) for j in range(MARGIN)
        ]
        rows = []
        for o in range(MARGIN):
            value = part_ref[o, :, lanes]
            for k, j in pairs_of(o):
                value = value + taps_ref[k : k + 1, lanes] * halo[j]
            rows.append(value.astype(BF))
        blocks.append(jnp.concatenate(rows, axis=0))
    return jnp.concatenate(blocks, axis=1)


def pair_4a(i):
    return i ^ 1


def pair_4b(i):
    return 3 - i


def pair_8a(i):
    return i ^ 1


def pair_8b(i):
    return (i + 1) % 8 if i % 2 else (i - 1) % 8


def pair_8c(i):
    return (3, 6, 5, 0, 7, 2, 1, 4)[i]


ROUNDS = [
    ("x", pair_4a), ("x", pair_4b), ("y", pair_4a), ("y", pair_4b),
    ("z", pair_8a), ("z", pair_8b), ("z", pair_8c),
]


def round_pairs(axis, rule):
    pairs = []
    for y in range(Y):
        for core in range(CORE):
            for z in range(Z):
                for x in range(X):
                    at = {"y": y, "core": core, "z": z, "x": x}
                    to = dict(at, core=1 - core)
                    to[axis] = rule(at[axis])
                    pairs.append(
                        tuple(((p["y"] * CORE + p["core"]) * Z + p["z"]) * X + p["x"] for p in (at, to))
                    )
    return pairs


def summed_over_all(mine, theirs):
    swap = [(0, 1), (1, 0)]
    total = mine + lax.ppermute(theirs, "core", swap).astype(F32)
    for axis, rule in ROUNDS:
        total = lax.optimization_barrier(total)
        got = lax.ppermute(total.astype(BF), ALL, round_pairs(axis, rule))
        total = total + got.astype(F32)
    return total, lax.ppermute(total, "core", swap)


def split3(a):
    hi = a.astype(BF)
    return hi, (a - hi.astype(F32)).astype(BF)


def dot(a, b, dims):
    return lax.dot_general(a, b, (dims, ((), ())), preferred_element_type=F32)


def dot3(a, b, dims):
    ah, al = split3(a)
    bh, bl = split3(b)
    return dot(ah, bh, dims) + (dot(ah, bl, dims) + dot(al, bh, dims))


NN = ((1,), (0,))
NT = ((1,), (1,))
TN = ((0,), (0,))


def coeffs_of(basis, coeffs, numerator):
    gram = dot3(basis, basis, NT)
    return coeffs * numerator / (dot3(gram, coeffs, NN) + EPS)


def emit_sums(half_ref, coeffs, feature, mine_ref, theirs_ref):
    c, rows = feature.shape[1], mine_ref.shape[0]
    first = half_ref[0] == 0
    num = dot(coeffs.astype(BF), feature, NN)
    mine_ref[:, :c] = jnp.where(first, num[:rows], num[rows:])
    theirs_ref[:, :c] = jnp.where(first, num[rows:], num[:rows]).astype(BF)
    gram = dot3(coeffs, coeffs, NT)
    gram = jnp.concatenate([gram, jnp.zeros_like(gram)], axis=1)
    mine_ref[:, c:] = jnp.where(first, gram[:rows], gram[rows:])
    theirs_ref[:, c:] = jnp.where(first, gram[rows:], gram[:rows]).astype(BF)


def first_kernel(
    flags_ref, mid_ref, top_ref, low_ref, above_ref, below_ref, taps_ref, w_ref, basis_ref,
    feature_ref, coeffs_ref, mine_ref, theirs_ref,
):
    rows, cols, channels = mid_ref.shape
    edge, mid = MARGIN * cols, rows * cols
    w = w_ref[...]
    top = finished_edge(
        top_ref, above_ref, taps_ref, flags_ref[3] == 1, lambda o: [(j - o, j) for j in range(o, MARGIN)]
    )
    low = finished_edge(
        low_ref, below_ref, taps_ref, flags_ref[4] == 1, lambda o: [(2 * MARGIN + j - o, j) for j in range(o + 1)]
    )

    def squeezed(mixed):
        return jnp.maximum(dot(mixed, w, NN), 0.0).astype(BF)

    feature_ref[:edge] = squeezed(top)
    feature_ref[edge : edge + mid] = squeezed(mid_ref[...].reshape(mid, channels))
    feature_ref[edge + mid :] = squeezed(low)
    feature = feature_ref[...]
    basis = basis_ref[...]
    scores = dot(basis.astype(BF), feature, NT)
    e = jnp.exp(scores - jnp.max(scores, axis=0, keepdims=True))
    soft = e / jnp.sum(e, axis=0, keepdims=True)
    coeffs = coeffs_of(basis, soft, scores)
    coeffs_ref[...] = coeffs
    emit_sums(flags_ref, coeffs, feature, mine_ref, theirs_ref)


def updated_basis(half_ref, own_ref, got_ref, basis):
    own, got = own_ref[...], got_ref[...]
    first = half_ref[0] == 0
    both = jnp.concatenate([jnp.where(first, own, got), jnp.where(first, got, own)], axis=0)
    r, c = basis.shape
    gram = both[:, c : c + r]
    return basis * both[:, :c] / (dot3(gram, basis, TN) + EPS)


def step_kernel(
    half_ref, own_ref, got_ref, basis_ref, feature_ref, coeffs_ref,
    newbasis_ref, newcoeffs_ref, mine_ref, theirs_ref,
):
    basis = updated_basis(half_ref, own_ref, got_ref, basis_ref[...])
    newbasis_ref[...] = basis
    feature = feature_ref[...]
    coeffs = coeffs_of(basis, coeffs_ref[...], dot(basis.astype(BF), feature, NT))
    newcoeffs_ref[...] = coeffs
    emit_sums(half_ref, coeffs, feature, mine_ref, theirs_ref)


def last_kernel(
    half_ref, own_ref, got_ref, basis_ref, feature_ref, coeffs_ref, wham_ref, walign_ref, out_ref
):
    basis = updated_basis(half_ref, own_ref, got_ref, basis_ref[...])
    feature = feature_ref[...]
    low = basis.astype(BF)
    coeffs = coeffs_of(basis, coeffs_ref[...], dot(low, feature, NT))
    rebuilt = dot(coeffs.astype(BF), low, TN).astype(BF)
    hammed = jnp.maximum(feature.astype(F32) + dot(rebuilt, wham_ref[...], NN), 0.0).astype(BF)
    out_ref[...] = dot(hammed, walign_ref[...], NN).astype(BF)


def call(kernel, outs, *args):
    scalar, whole = pl.BlockSpec(memory_space=pltpu.SMEM), pl.BlockSpec(memory_space=pltpu.VMEM)
    specs = [scalar if a.dtype == jnp.int32 else whole for a in args]
    return pl.pallas_call(
        kernel,
        out_shape=outs,
        in_specs=specs,
        out_specs=jax.tree.map(lambda _: pl.BlockSpec(memory_space=pltpu.VMEM), outs),
        compiler_params=pltpu.CompilerParams(vmem_limit_bytes=24 * 2**20),
    )(*args)


def on_device(band_input, column_taps, row_taps, w_squeeze, bases_init, w_ham, w_align):
    tile_rows, tile_cols, channels = band_input.shape
    margin = column_taps.shape[0] // 2
    index = {name: lax.axis_index(name) for name in ALL}
    half = sum(index.values()) % 2
    row, col = lax.axis_index(ROWS), lax.axis_index(COLS)
    flags = [half, col > 0, col < Z * X - 1, row > 0, row < Y * CORE - 1]
    flags = jnp.stack([f.astype(jnp.int32) for f in flags])
    sds = jax.ShapeDtypeStruct

    def ring(count, by):
        return [(i, (i + by) % count) for i in range(count)]

    rows_at_once = 16
    sent = pl.BlockSpec((margin, rows_at_once, channels), lambda i: (0, i, 0))
    right, left = pl.pallas_call(
        pack_kernel,
        grid=(tile_rows // rows_at_once,),
        in_specs=[pl.BlockSpec((rows_at_once, tile_cols, channels), lambda i: (i, 0, 0))],
        out_specs=[sent, sent],
        out_shape=[sds((margin, tile_rows, channels), BF)] * 2,
        scratch_shapes=[pltpu.VMEM((channels // LANES, rows_at_once * tile_cols, LANES), F32)],
        compiler_params=pltpu.CompilerParams(vmem_limit_bytes=58 * 2**20),
    )(band_input)
    left = lax.ppermute(left, COLS, ring(Z * X, 1))
    right = lax.ppermute(right, COLS, ring(Z * X, -1))

    def blocks(*dims):
        return pl.BlockSpec((*dims, LANES), lambda i: (*(0 for _ in dims), i))

    scalar = pl.BlockSpec(memory_space=pltpu.SMEM)
    tile = blocks(tile_rows, tile_cols)
    side, edge = blocks(margin, tile_rows), blocks(margin, tile_cols)
    taps = blocks(TAPS)
    grid = (channels // LANES,)
    flat = pltpu.VMEM((tile_rows * tile_cols, LANES), F32)
    params = pltpu.CompilerParams(vmem_limit_bytes=20 * 2**20)
    pixels = tile_rows * tile_cols * channels
    cost = pl.CostEstimate(flops=2 * TAPS * pixels, bytes_accessed=6 * pixels, transcendentals=0)
    own = pl.pallas_call(
        columns_own_kernel,
        grid=grid,
        in_specs=[tile, taps],
        out_specs=tile,
        out_shape=sds(band_input.shape, F32),
        scratch_shapes=[flat, pltpu.VMEM((tile_cols, tile_rows, LANES), F32)],
        compiler_params=params,
        cost_estimate=cost,
    )(band_input, column_taps)
    filtered = pl.pallas_call(
        columns_rest_kernel,
        grid=grid,
        in_specs=[scalar, tile, side, side, taps],
        out_specs=tile,
        out_shape=sds(band_input.shape, BF),
        scratch_shapes=[pltpu.VMEM((margin, tile_rows, LANES), F32)] * 2 + [flat],
        compiler_params=params,
    )(flags, own, left, right, column_taps)
    above = lax.ppermute(filtered[tile_rows - margin :], ROWS, ring(Y * CORE, 1))
    below = lax.ppermute(filtered[:margin], ROWS, ring(Y * CORE, -1))
    rest = tile_rows - 2 * margin
    mid, top, low = pl.pallas_call(
        rows_own_kernel,
        grid=grid,
        in_specs=[tile, tile, taps],
        out_specs=[blocks(rest, tile_cols), edge, edge],
        out_shape=[
            sds((rest, tile_cols, channels), BF),
            sds((margin, tile_cols, channels), F32),
            sds((margin, tile_cols, channels), F32),
        ],
        scratch_shapes=[
            pltpu.VMEM((tile_rows, tile_cols, LANES), F32),
            pltpu.VMEM((tile_rows, tile_cols, LANES), F32),
            pltpu.VMEM((rest, tile_cols, LANES), F32),
        ],
        compiler_params=params,
        cost_estimate=cost,
    )(filtered, band_input, row_taps)
    n, r = tile_rows * tile_cols, bases_init.shape[1]
    width = channels + 128
    sums = [sds((r // 2, width), F32), sds((r // 2, width), BF)]
    basis = bases_init.T
    feature, coeffs, mine, theirs = call(
        first_kernel,
        [sds((n, channels), BF), sds((r, n), F32)] + sums,
        flags, mid, top, low, above, below, row_taps, w_squeeze, basis,
    )
    for _ in range(STEPS - 1):
        own, got = summed_over_all(mine, theirs)
        basis, coeffs, mine, theirs = call(
            step_kernel,
            [sds((r, channels), F32), sds((r, n), F32)] + sums,
            flags, own, got, basis, feature, coeffs,
        )
    own, got = summed_over_all(mine, theirs)
    head_out = call(
        last_kernel,
        sds((n, channels), BF),
        flags, own, got, basis, feature, coeffs, w_ham, w_align,
    )
    return head_out.reshape(tile_rows, tile_cols, channels)


def solution(mesh):
    split = Mesh(mesh.devices.reshape(Y, CORE, Z, X), ALL)
    in_specs = (P(ROWS, COLS, None), P(), P(), P(), P(), P(), P())
    out_specs = P(ROWS, COLS, None)
    return jax.shard_map(
        on_device, mesh=split, in_specs=in_specs, out_specs=out_specs, check_vma=False
    )
```

```python
import jax
import jax.numpy as jnp
from jax import lax
from jax.experimental import pallas as pl
from jax.experimental.pallas import tpu as pltpu
from jax.sharding import Mesh
from jax.sharding import PartitionSpec as P

STEPS = 3
Y, CORE, Z, X = 4, 2, 8, 4
ROWS = ("y", "core")
COLS = ("z", "x")
ALL = ("y", "core", "z", "x")
EPS = 1e-06
BF = jnp.bfloat16
F32 = jnp.float32


TAPS = 21
MARGIN = TAPS // 2
LANES = 128


def weighted(taps_ref, items, rows):
    outs = [None] * len(items)
    for k in range(TAPS):
        if not any(k in pairs for pairs in items):
            continue
        tap = jnp.broadcast_to(taps_ref[k : k + 1, :], (rows, LANES))
        for i, pairs in enumerate(items):
            if k in pairs:
                term = tap * pairs[k]
                outs[i] = term if outs[i] is None else outs[i] + term
    return outs


def own_sums(taps_ref, load, length, group, emit):
    for start in range(0, length, group):
        lo, hi = max(0, start - MARGIN), min(length, start + group + MARGIN)
        window = {i: load(i) for i in range(lo, hi)}
        items = [
            {k: window[o + k - MARGIN] for k in range(TAPS) if o + k - MARGIN in window}
            for o in range(start, start + group)
        ]
        for i, value in enumerate(weighted(taps_ref, items, 8)):
            emit(start + i, value)


def columns_own_kernel(band_ref, taps_ref, out_ref, flat, turned):
    h, w, lanes = band_ref.shape
    flat[...] = band_ref[...].astype(F32).reshape(h * w, lanes)
    for j in range(w):
        turned[j] = flat[pl.ds(j, h, stride=w), :]

    def body(i, carry):
        rows = pl.ds(pl.multiple_of(i * 8, 8), 8)

        def emit(o, value):
            flat[pl.ds(i * (8 * w) + o, 8, stride=w), :] = value

        own_sums(taps_ref, lambda j: turned[j, rows, :], w, 8, emit)
        return carry

    lax.fori_loop(0, h // 8, body, 0)
    out_ref[...] = flat[...].reshape(h, w, lanes)


def columns_rest_kernel(flags_ref, own_ref, left_ref, right_ref, taps_ref, out_ref, lefts, rights, flat):
    h, w, lanes = own_ref.shape
    lefts[...] = jnp.where(flags_ref[1] == 1, left_ref[...].astype(F32), 0.0)
    rights[...] = jnp.where(flags_ref[2] == 1, right_ref[...].astype(F32), 0.0)

    @pl.when(pl.program_id(0) == 0)
    def _():
        flat[...] = jnp.zeros_like(flat)

    def body(i, carry):
        rows = pl.ds(pl.multiple_of(i * 8, 8), 8)

        def put(o, value):
            flat[pl.ds(i * (8 * w) + o, 8, stride=w), :] = value

        before = [lefts[j, rows, :] for j in range(MARGIN)]
        items = [{j - o: before[j] for j in range(o, MARGIN)} for o in range(MARGIN)]
        for o, value in enumerate(weighted(taps_ref, items, 8)):
            put(o, value)
        after = [rights[j, rows, :] for j in range(MARGIN)]
        items = [{2 * MARGIN + j - o: after[j] for j in range(o + 1)} for o in range(MARGIN)]
        for o, value in enumerate(weighted(taps_ref, items, 8)):
            put(w - MARGIN + o, value)
        return carry

    lax.fori_loop(0, h // 8, body, 0)
    out_ref[...] = (own_ref[...] + flat[...].reshape(h, w, lanes)).astype(BF)


def rows_own_kernel(filtered_ref, band_ref, taps_ref, mid_ref, top_ref, low_ref, source, residual, mixed):
    h, w, _ = filtered_ref.shape
    source[...] = filtered_ref[...].astype(F32)
    residual[...] = band_ref[...].astype(F32)

    def body(i, carry):
        cols = pl.ds(pl.multiple_of(i * 8, 8), 8)

        def emit(o, value):
            value = residual[o, cols, :] + value
            if o < MARGIN:
                top_ref[o, cols, :] = value
            elif o >= h - MARGIN:
                low_ref[o - (h - MARGIN), cols, :] = value
            else:
                mixed[o - MARGIN, cols, :] = value

        own_sums(taps_ref, lambda j: source[j, cols, :], h, 8, emit)
        return carry

    lax.fori_loop(0, w // 8, body, 0)
    mid_ref[...] = mixed[...].astype(BF)


def finished_edge(part_ref, halo_ref, taps_ref, present, pairs_of):
    blocks = []
    for start in range(0, part_ref.shape[2], LANES):
        lanes = slice(start, start + LANES)
        halo = [
            jnp.where(present, halo_ref[j, :, lanes].astype(F32), 0.0) for j in range(MARGIN)
        ]
        rows = []
        for o in range(MARGIN):
            value = part_ref[o, :, lanes]
            for k, j in pairs_of(o):
                value = value + taps_ref[k : k + 1, lanes] * halo[j]
            rows.append(value.astype(BF))
        blocks.append(jnp.concatenate(rows, axis=0))
    return jnp.concatenate(blocks, axis=1)


def pair_4a(i):
    return i ^ 1


def pair_4b(i):
    return 3 - i


def pair_8a(i):
    return i ^ 1


def pair_8b(i):
    return (i + 1) % 8 if i % 2 else (i - 1) % 8


def pair_8c(i):
    return (3, 6, 5, 0, 7, 2, 1, 4)[i]


ROUNDS = [
    ("z", pair_8a), ("z", pair_8b), ("z", pair_8c),
    ("y", pair_4b), ("y", pair_4a), ("x", pair_4b), ("x", pair_4a),
]


def round_pairs(axis, rule):
    pairs = []
    for y in range(Y):
        for core in range(CORE):
            for z in range(Z):
                for x in range(X):
                    at = {"y": y, "core": core, "z": z, "x": x}
                    to = dict(at, core=1 - core)
                    to[axis] = rule(at[axis])
                    pairs.append(
                        tuple(((p["y"] * CORE + p["core"]) * Z + p["z"]) * X + p["x"] for p in (at, to))
                    )
    return pairs


def summed_over_all(mine, theirs):
    swap = [(0, 1), (1, 0)]
    total = mine + lax.ppermute(theirs, "core", swap).astype(F32)
    for axis, rule in ROUNDS:
        total = lax.optimization_barrier(total)
        got = lax.ppermute(total.astype(BF), ALL, round_pairs(axis, rule))
        total = total + got.astype(F32)
    return total, lax.ppermute(total, "core", swap)


def split3(a):
    hi = a.astype(BF)
    return hi, (a - hi.astype(F32)).astype(BF)


def dot(a, b, dims):
    return lax.dot_general(a, b, (dims, ((), ())), preferred_element_type=F32)


def dot3(a, b, dims):
    ah, al = split3(a)
    bh, bl = split3(b)
    return dot(ah, bh, dims) + (dot(ah, bl, dims) + dot(al, bh, dims))


NN = ((1,), (0,))
NT = ((1,), (1,))
TN = ((0,), (0,))


def coeffs_of(basis, coeffs, numerator):
    gram = dot3(basis, basis, NT)
    return coeffs * numerator / (dot3(gram, coeffs, NN) + EPS)


def emit_sums(half_ref, coeffs, feature, mine_ref, theirs_ref):
    c, rows = feature.shape[1], mine_ref.shape[0]
    first = half_ref[0] == 0
    num = dot(coeffs.astype(BF), feature, NN)
    mine_ref[:, :c] = jnp.where(first, num[:rows], num[rows:])
    theirs_ref[:, :c] = jnp.where(first, num[rows:], num[:rows]).astype(BF)
    gram = dot3(coeffs, coeffs, NT)
    gram = jnp.concatenate([gram, jnp.zeros_like(gram)], axis=1)
    mine_ref[:, c:] = jnp.where(first, gram[:rows], gram[rows:])
    theirs_ref[:, c:] = jnp.where(first, gram[rows:], gram[:rows]).astype(BF)


def first_kernel(
    flags_ref, mid_ref, top_ref, low_ref, above_ref, below_ref, taps_ref, w_ref, basis_ref,
    feature_ref, coeffs_ref, mine_ref, theirs_ref,
):
    rows, cols, channels = mid_ref.shape
    edge, mid = MARGIN * cols, rows * cols
    w = w_ref[...]
    top = finished_edge(
        top_ref, above_ref, taps_ref, flags_ref[3] == 1, lambda o: [(j - o, j) for j in range(o, MARGIN)]
    )
    low = finished_edge(
        low_ref, below_ref, taps_ref, flags_ref[4] == 1, lambda o: [(2 * MARGIN + j - o, j) for j in range(o + 1)]
    )

    def squeezed(mixed):
        return jnp.maximum(dot(mixed, w, NN), 0.0).astype(BF)

    feature_ref[:edge] = squeezed(top)
    feature_ref[edge : edge + mid] = squeezed(mid_ref[...].reshape(mid, channels))
    feature_ref[edge + mid :] = squeezed(low)
    feature = feature_ref[...]
    basis = basis_ref[...]
    scores = dot(basis.astype(BF), feature, NT)
    e = jnp.exp(scores - jnp.max(scores, axis=0, keepdims=True))
    soft = e / jnp.sum(e, axis=0, keepdims=True)
    coeffs = coeffs_of(basis, soft, scores)
    coeffs_ref[...] = coeffs
    emit_sums(flags_ref, coeffs, feature, mine_ref, theirs_ref)


def updated_basis(half_ref, own_ref, got_ref, basis):
    own, got = own_ref[...], got_ref[...]
    first = half_ref[0] == 0
    both = jnp.concatenate([jnp.where(first, own, got), jnp.where(first, got, own)], axis=0)
    r, c = basis.shape
    gram = both[:, c : c + r]
    return basis * both[:, :c] / (dot3(gram, basis, TN) + EPS)


def step_kernel(
    half_ref, own_ref, got_ref, basis_ref, feature_ref, coeffs_ref,
    newbasis_ref, newcoeffs_ref, mine_ref, theirs_ref,
):
    basis = updated_basis(half_ref, own_ref, got_ref, basis_ref[...])
    newbasis_ref[...] = basis
    feature = feature_ref[...]
    coeffs = coeffs_of(basis, coeffs_ref[...], dot(basis.astype(BF), feature, NT))
    newcoeffs_ref[...] = coeffs
    emit_sums(half_ref, coeffs, feature, mine_ref, theirs_ref)


def last_kernel(
    half_ref, own_ref, got_ref, basis_ref, feature_ref, coeffs_ref, wham_ref, walign_ref, out_ref
):
    basis = updated_basis(half_ref, own_ref, got_ref, basis_ref[...])
    feature = feature_ref[...]
    low = basis.astype(BF)
    coeffs = coeffs_of(basis, coeffs_ref[...], dot(low, feature, NT))
    rebuilt = dot(coeffs.astype(BF), low, TN).astype(BF)
    hammed = jnp.maximum(feature.astype(F32) + dot(rebuilt, wham_ref[...], NN), 0.0).astype(BF)
    out_ref[...] = dot(hammed, walign_ref[...], NN).astype(BF)


def call(kernel, outs, *args):
    scalar, whole = pl.BlockSpec(memory_space=pltpu.SMEM), pl.BlockSpec(memory_space=pltpu.VMEM)
    specs = [scalar if a.dtype == jnp.int32 else whole for a in args]
    return pl.pallas_call(
        kernel,
        out_shape=outs,
        in_specs=specs,
        out_specs=jax.tree.map(lambda _: pl.BlockSpec(memory_space=pltpu.VMEM), outs),
        compiler_params=pltpu.CompilerParams(vmem_limit_bytes=24 * 2**20),
    )(*args)


def on_device(band_input, column_taps, row_taps, w_squeeze, bases_init, w_ham, w_align):
    tile_rows, tile_cols, channels = band_input.shape
    margin = column_taps.shape[0] // 2
    index = {name: lax.axis_index(name) for name in ALL}
    half = sum(index.values()) % 2
    row, col = lax.axis_index(ROWS), lax.axis_index(COLS)
    flags = [half, col > 0, col < Z * X - 1, row > 0, row < Y * CORE - 1]
    flags = jnp.stack([f.astype(jnp.int32) for f in flags])
    sds = jax.ShapeDtypeStruct

    def ring(count, by):
        return [(i, (i + by) % count) for i in range(count)]

    left = band_input[:, tile_cols - margin :].transpose(1, 0, 2)
    right = band_input[:, :margin].transpose(1, 0, 2)
    left = lax.ppermute(left, COLS, ring(Z * X, 1))
    right = lax.ppermute(right, COLS, ring(Z * X, -1))

    def blocks(*dims):
        return pl.BlockSpec((*dims, LANES), lambda i: (*(0 for _ in dims), i))

    scalar = pl.BlockSpec(memory_space=pltpu.SMEM)
    tile = blocks(tile_rows, tile_cols)
    side, edge = blocks(margin, tile_rows), blocks(margin, tile_cols)
    taps = blocks(TAPS)
    grid = (channels // LANES,)
    flat = pltpu.VMEM((tile_rows * tile_cols, LANES), F32)
    params = pltpu.CompilerParams(vmem_limit_bytes=20 * 2**20)
    pixels = tile_rows * tile_cols * channels
    cost = pl.CostEstimate(flops=2 * TAPS * pixels, bytes_accessed=6 * pixels, transcendentals=0)
    own = pl.pallas_call(
        columns_own_kernel,
        grid=grid,
        in_specs=[tile, taps],
        out_specs=tile,
        out_shape=sds(band_input.shape, F32),
        scratch_shapes=[flat, pltpu.VMEM((tile_cols, tile_rows, LANES), F32)],
        compiler_params=params,
        cost_estimate=cost,
    )(band_input, column_taps)
    filtered = pl.pallas_call(
        columns_rest_kernel,
        grid=grid,
        in_specs=[scalar, tile, side, side, taps],
        out_specs=tile,
        out_shape=sds(band_input.shape, BF),
        scratch_shapes=[pltpu.VMEM((margin, tile_rows, LANES), F32)] * 2 + [flat],
        compiler_params=params,
    )(flags, own, left, right, column_taps)
    above = lax.ppermute(filtered[tile_rows - margin :], ROWS, ring(Y * CORE, 1))
    below = lax.ppermute(filtered[:margin], ROWS, ring(Y * CORE, -1))
    rest = tile_rows - 2 * margin
    mid, top, low = pl.pallas_call(
        rows_own_kernel,
        grid=grid,
        in_specs=[tile, tile, taps],
        out_specs=[blocks(rest, tile_cols), edge, edge],
        out_shape=[
            sds((rest, tile_cols, channels), BF),
            sds((margin, tile_cols, channels), F32),
            sds((margin, tile_cols, channels), F32),
        ],
        scratch_shapes=[
            pltpu.VMEM((tile_rows, tile_cols, LANES), F32),
            pltpu.VMEM((tile_rows, tile_cols, LANES), F32),
            pltpu.VMEM((rest, tile_cols, LANES), F32),
        ],
        compiler_params=params,
        cost_estimate=cost,
    )(filtered, band_input, row_taps)
    n, r = tile_rows * tile_cols, bases_init.shape[1]
    width = channels + 128
    sums = [sds((r // 2, width), F32), sds((r // 2, width), BF)]
    basis = bases_init.T
    feature, coeffs, mine, theirs = call(
        first_kernel,
        [sds((n, channels), BF), sds((r, n), F32)] + sums,
        flags, mid, top, low, above, below, row_taps, w_squeeze, basis,
    )
    for _ in range(STEPS - 1):
        own, got = summed_over_all(mine, theirs)
        basis, coeffs, mine, theirs = call(
            step_kernel,
            [sds((r, channels), F32), sds((r, n), F32)] + sums,
            flags, own, got, basis, feature, coeffs,
        )
    own, got = summed_over_all(mine, theirs)
    head_out = call(
        last_kernel,
        sds((n, channels), BF),
        flags, own, got, basis, feature, coeffs, w_ham, w_align,
    )
    return head_out.reshape(tile_rows, tile_cols, channels)


def solution(mesh):
    split = Mesh(mesh.devices.reshape(Y, CORE, Z, X), ALL)
    in_specs = (P(ROWS, COLS, None), P(), P(), P(), P(), P(), P())
    out_specs = P(ROWS, COLS, None)
    return jax.shard_map(
        on_device, mesh=split, in_specs=in_specs, out_specs=out_specs, check_vma=False
    )
```
